256 devices in a mesh: level: 32 (over x, z), slab: 8 (over y, core).
Axes of the slice: x: 4, y: 4, z: 8, core: 2. Of those that a mesh axis runs over, the one named last changes fastest.
Arguments:
- trajectory: float32 [32, 8, 16, 32, 128], P('level', None, 'slab'), may hold values from -6 to 6
- first_latent: float32 [8, 16, 32, 128], P(None, 'slab'), may hold values from -6 to 6
- noise_draw: float32 [32, 8, 16, 32, 128], P('level', None, 'slab'), may hold values from -6 to 6
- w_in: bfloat16 [64, 8, 3, 3, 3], replicated, may hold values from -0.4375 to 0.4375
- bias_in: float32 [64], replicated, may hold values from -3 to 3
- level_bias: float32 [32, 64], P('level'), may hold values from -3 to 3
- w_out: bfloat16 [8, 64, 3, 3, 3], replicated, may hold values from -0.15625 to 0.15625
- bias_out: float32 [8], replicated, may hold values from -2 to 2
- drift_coef: float32 [32], P('level'), may hold values from -0.12 to -0.02
- eps_coef: float32 [32], P('level'), may hold values from 0.05 to 0.3
- noise_coef: float32 [32], P('level'), may hold values from 0.05 to 0.2
Outputs:
- next_states: float32 [32, 8, 16, 32, 128], P('level', None, 'slab')
The draws below stay inside these ranges and needn't reach their ends.
All inputs are finite; a program needn't handle non-finite values.
Results may differ from the reference program's by a relative error of at most 0.0016.
Values may be sent and summed in bfloat16 or wider, within the bound.
No kernel may reach another device: no remote copies, remote signals or barrier semaphores. Data moves between devices by JAX's collectives and lax.ppermute only.
A program may use at most 64 MiB of HBM per device.

```python
import math
import jax
import jax.numpy as jnp
from jax import lax

C = 8
HID = 64
H = 32
W = 128
ITERS = 2
LEVELS = 32
NZ = 16


def block_scale(own_key, dims, shards, smallest, top_value):
    def one(dim, shards_of):
        draws = jax.random.uniform(jax.random.fold_in(jax.random.fold_in(own_key, 6), dim), (shards_of,), jnp.float32, smallest / len(shards), top_value / len(shards))
        return jnp.repeat(jnp.exp(draws), dims[dim] // shards_of).reshape((-1,) + (1,) * (len(dims) - dim - 1))

    level = one(*shards[0])
    for cut in shards[1:]:
        level = level * one(*cut)
    return level


def gaussian(key, extent, spread, most, cuts=(), held_as=jnp.bfloat16):
    values = spread * jax.random.normal(key, extent, jnp.float32)
    if cuts:
        values = values * block_scale(key, extent, cuts, -0.22, 0.18)
    return jnp.clip(values, -most, most).astype(held_as)


def setup_inputs(seed: int = 0) -> dict:
    key_list = jax.random.split(jax.random.key(seed), 12)
    return {
        "trajectory": gaussian(key_list[0], (LEVELS, C, NZ, H, W), 1.0, 6.0, ((0, 32), (2, 8)), jnp.float32),
        "first_latent": gaussian(key_list[1], (C, NZ, H, W), 1.0, 6.0, ((1, 8),), jnp.float32),
        "noise_draw": gaussian(key_list[2], (LEVELS, C, NZ, H, W), 1.0, 6.0, ((0, 32), (2, 8)), jnp.float32),
        "w_in": gaussian(key_list[3], (HID, C, 3, 3, 3), (C * 27) ** -0.5, 0.4375),
        "bias_in": gaussian(key_list[4], (HID,), 0.5, 3.0, (), jnp.float32),
        "level_bias": gaussian(key_list[5], (LEVELS, HID), 0.5, 3.0, ((0, 32),), jnp.float32),
        "w_out": gaussian(key_list[6], (C, HID, 3, 3, 3), (HID * 27) ** -0.5, 0.15625),
        "bias_out": gaussian(key_list[7], (C,), 0.3, 2.0, (), jnp.float32),
        "drift_coef": jnp.clip(-0.12 + 0.09999999776482582 * jax.random.uniform(key_list[8], (LEVELS,), jnp.float32) ** block_scale(key_list[8], (LEVELS,), ((0, 32),), -0.2, 0.2), -0.12, -0.02),
        "eps_coef": jnp.clip(jnp.exp(math.log(0.3) - 1.7917595 * jax.random.uniform(key_list[9], (LEVELS,), jnp.float32) ** block_scale(key_list[9], (LEVELS,), ((0, 32),), -0.2, 0.2)), 0.05, 0.3),
        "noise_coef": jnp.clip(jnp.exp(math.log(0.2) - 1.3862944 * jax.random.uniform(key_list[10], (LEVELS,), jnp.float32) ** block_scale(key_list[10], (LEVELS,), ((0, 32),), -0.2, 0.2)), 0.05, 0.2),
    }


def convolve(field, kernel):
    return lax.conv_general_dilated(field[None].astype(jnp.float32), kernel.astype(jnp.float32), (1, 1, 1), ((1, 1), (1, 1), (1, 1)), dimension_numbers=("NCDHW", "OIDHW", "NCDHW"), precision=lax.Precision.HIGHEST)[0]


def reference(trajectory, first_latent, noise_draw, w_in, bias_in, level_bias, w_out, bias_out, drift_coef, eps_coef, noise_coef):
    def level_step(items):
        current, fresh, level_row, drift, scale_eps, scale_noise = items
        latent_bf = current.astype(jnp.bfloat16)
        before = convolve(latent_bf, w_in)
        hidden = jax.nn.silu(before + (bias_in + level_row)[:, None, None, None]).astype(jnp.bfloat16)
        predicted = convolve(hidden, w_out) + bias_out[:, None, None, None]
        return drift * current + scale_eps * predicted + scale_noise * fresh

    states = trajectory
    result = trajectory
    for step in range(ITERS):
        increment = lax.map(level_step, (states, noise_draw, level_bias, drift_coef, eps_coef, noise_coef))
        inclusive = jnp.cumsum(increment, axis=0)
        if step + 1 < ITERS:
            shifted = jnp.concatenate([jnp.zeros_like(inclusive[:1]), inclusive[:-1]], axis=0)
            states = first_latent[None] + shifted
        else:
            result = first_latent[None] + inclusive
    return result
```

```python
import jax
import jax.numpy as jnp
from jax import lax
from jax.experimental import pallas as pl
from jax.experimental.pallas import tpu as pltpu
from jax.sharding import PartitionSpec as P

C, HID, H, W = 8, 64, 32, 128
BF, F32 = jnp.bfloat16, jnp.float32
ROWS = (H * C, 2 * W)


def swapped(ref, plane, block):
    tile = ref[:, plane, block * 8 : block * 8 + 8, :]
    return jnp.swapaxes(tile, 0, 1).reshape(64, W)


def tiles():
    for plane in range(2):
        for block in range(4):
            yield plane, block, slice(block * 64, block * 64 + 64), slice(plane * W, plane * W + W)


def latent_kernel(x_ref, out_ref):
    for plane, block, rows, lanes in tiles():
        out_ref[rows, lanes] = swapped(x_ref, plane, block).astype(BF)


def prepare_kernel(
    eps, scale, noise_ref, first_ref, w_in_ref, bias_in_ref, level_bias_ref, w_out_ref, bias_out_ref,
    fresh_ref, start_ref, kernel_in_ref, kernel_out_ref, first,
):
    same = lax.broadcasted_iota(jnp.int32, (C, C), 0) == lax.broadcasted_iota(jnp.int32, (C, C), 1)
    column = jnp.sum(jnp.where(same, jnp.broadcast_to(bias_out_ref[...], (C, C)), 0.0), axis=1, keepdims=True)
    shift = jnp.concatenate([jnp.broadcast_to(eps[0] * column, (C, W))] * 8, axis=0)
    for plane, block, rows, lanes in tiles():
        fresh_ref[rows, lanes] = scale[0] * swapped(noise_ref, plane, block) + shift
        first[rows, lanes] = swapped(first_ref, plane, block)
    own = pl.multiple_of(lax.axis_index("level") * C, C)
    start_ref[...] = first[pl.ds(own, C), :]

    bias = 0.5 * (bias_in_ref[...] + level_bias_ref[...])
    high = bias.astype(BF).astype(F32)
    middle = (bias - high).astype(BF).astype(F32)
    low = bias - high - middle
    nothing = jnp.zeros((C, HID), F32)
    row = lax.broadcasted_iota(jnp.int32, (C, HID), 0)
    biases = jnp.where(row == 0, high, jnp.where(row == 1, middle, jnp.where(row == 2, low, 0.0)))
    pieces = []
    for kh in range(3):
        pieces += [0.5 * w_in_ref[kd * 9 + kh * 3 + kw].astype(F32) for kd in range(3) for kw in range(3)]
        pieces.append(biases if kh == 1 else nothing)
    stacked = jnp.concatenate(pieces + [nothing] * 2, axis=0)
    stacked = jnp.concatenate([stacked, jnp.zeros_like(stacked)], axis=1)
    kernel_in_ref[...] = stacked.T[:HID, :240].astype(BF)
    rows_of = [
        jnp.concatenate([w_out_ref[kd * 9 + kh * 3 + kw].astype(F32) for kd in range(3) for kw in range(3)], axis=0)
        for kh in range(3)
    ]
    kernel_out_ref[...] = jnp.concatenate(rows_of, axis=1).astype(BF)


def edge_masks():
    lane = lax.broadcasted_iota(jnp.int32, (8, W), 1)
    return lane > 0, lane < W - 1


def from_left(tile, keep):
    return jnp.where(keep, pltpu.roll(tile, 1, 1), 0.0)


def from_right(tile, keep):
    return jnp.where(keep, pltpu.roll(tile, W - 1, 1), 0.0)


def taps_of(row, keeps):
    blocks = [row[:, p * W : p * W + W] for p in range(6)]
    shifted = (
        [from_left(b, keeps[0]) for b in blocks],
        blocks,
        [from_right(b, keeps[1]) for b in blocks],
    )
    pieces = [jnp.concatenate(shifted[kw][kd : kd + 4], axis=1) for kd in range(3) for kw in range(3)]
    pieces.append(jnp.ones((C, 4 * W), F32))
    return jnp.concatenate(pieces, axis=0).astype(BF)


def hidden_of(taps, kernel_in, inside):
    u = jnp.dot(kernel_in, taps, preferred_element_type=F32)
    u = jnp.concatenate([u[:, :W] * inside[0], u[:, W : 3 * W], u[:, 3 * W :] * inside[1]], axis=1)
    return (u + u * jnp.tanh(u)).astype(BF)


def predicted_of(hidden, kernel_out, keeps):
    y = jnp.dot(kernel_out, hidden, preferred_element_type=F32)
    planes = []
    for plane in range(2):
        sums = []
        for kw in range(3):
            parts = [
                y[(kd * 3 + kw) * C : (kd * 3 + kw) * C + C, (plane + kd) * W : (plane + kd) * W + W]
                for kd in range(3)
            ]
            sums.append(parts[0] + parts[1] + parts[2])
        planes.append(sums[1] + from_left(sums[0], keeps[0]) + from_right(sums[2], keeps[1]))
    return jnp.concatenate(planes, axis=1)


def step_kernel(
    slabs, drift, eps, below_ref, latent_ref, above_ref, kernel_in_ref, kernel_out_ref, fresh_ref,
    inc_ref, taps, hidden,
):
    keeps = edge_masks()
    slab = lax.axis_index("slab")
    inside = (jnp.where(slab > 0, 1.0, 0.0).astype(F32), jnp.where(slab < slabs - 1, 1.0, 0.0).astype(F32))
    kernel_in, kernel_out = kernel_in_ref[...], kernel_out_ref[...]
    ones = jnp.concatenate([jnp.zeros((72, 4 * W), F32), jnp.ones((8, 4 * W), F32)], axis=0).astype(BF)
    for edge in (0, H + 1):
        taps[edge] = ones
        hidden[edge] = jnp.zeros((HID, 4 * W), BF)

    def load(pair):
        rows = slice(pair * 16, pair * 16 + 16)
        for k in range(2):
            refs = (below_ref, latent_ref, above_ref)
            both = jnp.concatenate([ref[rows, :].astype(F32) for ref in refs], axis=1)
            taps[1 + pair * 2 + k] = taps_of(both[k * C : k * C + C], keeps)

    def widen(row):
        hidden[1 + row] = hidden_of(taps[row : row + 3].reshape(240, 4 * W), kernel_in, inside)

    def narrow(row):
        pred = predicted_of(hidden[row : row + 3].reshape(3 * HID, 4 * W), kernel_out, keeps)
        rows = slice(row * C, row * C + C)
        pair = latent_ref[row // 2 * 16 : row // 2 * 16 + 16, :].astype(F32)
        state = pair[row % 2 * C : row % 2 * C + C]
        inc_ref[rows, :] = (drift[0] * state + fresh_ref[rows, :] + eps[0] * pred).astype(inc_ref.dtype)

    for beat in range(H // 2 + 4):
        if beat < H // 2:
            load(beat)
        if 0 <= beat - 2 < H // 2:
            widen(2 * (beat - 2))
            widen(2 * (beat - 2) + 1)
        if 0 <= beat - 4:
            narrow(2 * (beat - 4))
            narrow(2 * (beat - 4) + 1)


def scan_kernel(inclusive, x_ref, start_ref, out_ref):
    total = start_ref[...]
    for pair in range(16):
        rows = slice(pair * 16, pair * 16 + 16)
        both = x_ref[rows, :].astype(F32)
        middle = total + both[:C]
        after = middle + both[C:]
        kept = [middle, after] if inclusive else [total, middle]
        out_ref[rows, :] = jnp.concatenate(kept, axis=0).astype(out_ref.dtype)
        total = after


def final_kernel(state_ref, out_ref):
    for plane, block, rows, lanes in tiles():
        out_ref[:, plane, block * 8 : block * 8 + 8, :] = jnp.swapaxes(state_ref[rows, lanes].reshape(8, C, W), 0, 1)


VMEM = pl.BlockSpec(memory_space=pltpu.VMEM)
SMEM = pl.BlockSpec(memory_space=pltpu.SMEM)


def near(array):
    return pltpu.with_memory_space_constraint(array, pltpu.VMEM)


def call(kernel, scalars, arrays, outs, scratch=(), name=None):
    return pl.pallas_call(
        kernel,
        out_shape=outs if len(outs) > 1 else outs[0],
        in_specs=[SMEM] * len(scalars) + [VMEM] * len(arrays),
        out_specs=[VMEM] * len(outs) if len(outs) > 1 else VMEM,
        scratch_shapes=scratch,
        name=name,
    )(*scalars, *arrays)


def on_device(trajectory, first_latent, noise_draw, w_in, bias_in, level_bias, w_out, bias_out, drift, eps, scale):
    slabs = lax.axis_size("slab")
    levels = lax.axis_size("level")
    up = [(i, i + 1) for i in range(slabs - 1)]
    down = [(i + 1, i) for i in range(slabs - 1)]

    latent = call(latent_kernel, (), (trajectory[0],), [pltpu.VMEM(ROWS, BF)], name="latent")
    fresh, start, kernel_in, kernel_out = call(
        prepare_kernel,
        (eps, scale),
        (
            noise_draw[0], first_latent,
            jnp.transpose(w_in, (2, 3, 4, 1, 0)).reshape(27, C, HID), bias_in[None], level_bias,
            jnp.transpose(w_out, (2, 3, 4, 0, 1)).reshape(27, C, HID), bias_out[None],
        ),
        [pltpu.VMEM(ROWS, F32), pltpu.VMEM((C, 2 * W), F32), pltpu.VMEM((HID, 240), BF), pltpu.VMEM((72, 3 * HID), BF)],
        [pltpu.VMEM(ROWS, F32)],
        name="prepare",
    )

    def step(latent, sent):
        below = lax.ppermute(latent, "slab", up)
        above = lax.ppermute(latent, "slab", down)
        inc = call(
            lambda *refs: step_kernel(slabs, *refs),
            (drift, eps),
            [near(a) for a in (below, latent, above, kernel_in, kernel_out, fresh)],
            [pltpu.VMEM(ROWS, sent)],
            [pltpu.VMEM((H + 2, 80, 4 * W), BF), pltpu.VMEM((H + 2, HID, 4 * W), BF)],
            name="step",
        )
        return exchange(inc)

    def exchange(array):
        return lax.all_to_all(array.reshape(levels, -1, 2 * W), "level", 0, 0).reshape(ROWS)

    def scan(inc, inclusive, kept):
        out = call(
            lambda *refs: scan_kernel(inclusive, *refs), (), [near(inc), near(start)], [pltpu.VMEM(ROWS, kept)], name="scan"
        )
        return exchange(out)

    latent = scan(step(latent, F32), False, BF)
    state = scan(step(latent, BF), True, F32)
    return call(final_kernel, (), (near(state),), [jax.ShapeDtypeStruct((C, 2, H, W), F32)], name="final")[None]


def solution(mesh):
    placed = (
        P("level", None, "slab", None, None),
        P(None, "slab", None, None),
        P("level", None, "slab", None, None),
        P(),
        P(),
        P("level", None),
        P(),
        P(),
        P("level"),
        P("level"),
        P("level"),
    )
    return jax.shard_map(
        on_device,
        mesh=mesh,
        in_specs=placed,
        out_specs=P("level", None, "slab", None, None),
        check_vma=False,
    )
```

```python
import jax
import jax.numpy as jnp
from jax import lax
from jax.experimental import pallas as pl
from jax.experimental.pallas import tpu as pltpu
from jax.sharding import PartitionSpec as P

C, HID, H, W = 8, 64, 32, 128
BF, F32 = jnp.bfloat16, jnp.float32
ROWS = (H * C, 2 * W)


def swapped(ref, plane, block):
    tile = ref[:, plane, block * 8 : block * 8 + 8, :]
    return jnp.swapaxes(tile, 0, 1).reshape(64, W)


def tiles():
    for plane in range(2):
        for block in range(4):
            yield plane, block, slice(block * 64, block * 64 + 64), slice(plane * W, plane * W + W)


def latent_kernel(x_ref, out_ref):
    for plane, block, rows, lanes in tiles():
        out_ref[rows, lanes] = swapped(x_ref, plane, block).astype(BF)


def prepare_kernel(
    eps, scale, noise_ref, first_ref, w_in_ref, bias_in_ref, level_bias_ref, w_out_ref, bias_out_ref,
    fresh_ref, start_ref, kernel_in_ref, kernel_out_ref, first,
):
    same = lax.broadcasted_iota(jnp.int32, (C, C), 0) == lax.broadcasted_iota(jnp.int32, (C, C), 1)
    column = jnp.sum(jnp.where(same, jnp.broadcast_to(bias_out_ref[...], (C, C)), 0.0), axis=1, keepdims=True)
    shift = jnp.concatenate([jnp.broadcast_to(eps[0] * column, (C, W))] * 8, axis=0)
    for plane, block, rows, lanes in tiles():
        fresh_ref[rows, lanes] = scale[0] * swapped(noise_ref, plane, block) + shift
        first[rows, lanes] = swapped(first_ref, plane, block)
    own = pl.multiple_of(lax.axis_index("level") * C, C)
    start_ref[...] = first[pl.ds(own, C), :]

    bias = 0.5 * (bias_in_ref[...] + level_bias_ref[...])
    high = bias.astype(BF).astype(F32)
    middle = (bias - high).astype(BF).astype(F32)
    low = bias - high - middle
    nothing = jnp.zeros((C, HID), F32)
    row = lax.broadcasted_iota(jnp.int32, (C, HID), 0)
    biases = jnp.where(row == 0, high, jnp.where(row == 1, middle, jnp.where(row == 2, low, 0.0)))
    pieces = []
    for kh in range(3):
        pieces += [0.5 * w_in_ref[kd * 9 + kh * 3 + kw].astype(F32) for kd in range(3) for kw in range(3)]
        pieces.append(biases if kh == 1 else nothing)
    stacked = jnp.concatenate(pieces + [nothing] * 2, axis=0)
    stacked = jnp.concatenate([stacked, jnp.zeros_like(stacked)], axis=1)
    kernel_in_ref[...] = stacked.T[:HID, :240].astype(BF)
    rows_of = [
        jnp.concatenate([w_out_ref[kd * 9 + kh * 3 + kw].astype(F32) for kd in range(3) for kw in range(3)], axis=0)
        for kh in range(3)
    ]
    kernel_out_ref[...] = jnp.concatenate(rows_of, axis=1).astype(BF)


def edge_masks():
    lane = lax.broadcasted_iota(jnp.int32, (8, W), 1)
    return lane > 0, lane < W - 1


def from_left(tile, keep):
    return jnp.where(keep, pltpu.roll(tile, 1, 1), 0.0)


def from_right(tile, keep):
    return jnp.where(keep, pltpu.roll(tile, W - 1, 1), 0.0)


def taps_of(row, keeps):
    blocks = [row[:, p * W : p * W + W] for p in range(6)]
    shifted = (
        [from_left(b, keeps[0]) for b in blocks],
        blocks,
        [from_right(b, keeps[1]) for b in blocks],
    )
    pieces = [jnp.concatenate(shifted[kw][kd : kd + 4], axis=1) for kd in range(3) for kw in range(3)]
    pieces.append(jnp.ones((C, 4 * W), F32))
    return jnp.concatenate(pieces, axis=0).astype(BF)


def hidden_of(taps, kernel_in, inside):
    u = jnp.dot(kernel_in, taps, preferred_element_type=F32)
    u = jnp.concatenate([u[:, :W] * inside[0], u[:, W : 3 * W], u[:, 3 * W :] * inside[1]], axis=1)
    return (u + u * jnp.tanh(u)).astype(BF)


def predicted_of(hidden, kernel_out, keeps):
    y = jnp.dot(kernel_out, hidden, preferred_element_type=F32)
    planes = []
    for plane in range(2):
        sums = []
        for kw in range(3):
            parts = [
                y[(kd * 3 + kw) * C : (kd * 3 + kw) * C + C, (plane + kd) * W : (plane + kd) * W + W]
                for kd in range(3)
            ]
            sums.append(parts[0] + parts[1] + parts[2])
        planes.append(sums[1] + from_left(sums[0], keeps[0]) + from_right(sums[2], keeps[1]))
    return jnp.concatenate(planes, axis=1)


def step_kernel(
    slabs, drift, eps, paired_ref, latent_ref, crossed_ref, kernel_in_ref, kernel_out_ref, fresh_ref,
    inc_ref, taps, hidden,
):
    keeps = edge_masks()
    slab = lax.axis_index("slab")
    odd = slab % 2 == 1
    inside = (jnp.where(slab > 0, 1.0, 0.0).astype(F32), jnp.where(slab < slabs - 1, 1.0, 0.0).astype(F32))
    kernel_in, kernel_out = kernel_in_ref[...], kernel_out_ref[...]
    ones = jnp.concatenate([jnp.zeros((72, 4 * W), F32), jnp.ones((8, 4 * W), F32)], axis=0).astype(BF)
    for edge in (0, H + 1):
        taps[edge] = ones
        hidden[edge] = jnp.zeros((HID, 4 * W), BF)

    def load(pair):
        rows = slice(pair * 16, pair * 16 + 16)
        paired, crossed = paired_ref[rows, :].astype(F32), crossed_ref[rows, :].astype(F32)
        below, above = jnp.where(odd, paired, crossed), jnp.where(odd, crossed, paired)
        both = jnp.concatenate([below, latent_ref[rows, :].astype(F32), above], axis=1)
        for k in range(2):
            taps[1 + pair * 2 + k] = taps_of(both[k * C : k * C + C], keeps)

    def widen(row):
        hidden[1 + row] = hidden_of(taps[row : row + 3].reshape(240, 4 * W), kernel_in, inside)

    def narrow(row):
        pred = predicted_of(hidden[row : row + 3].reshape(3 * HID, 4 * W), kernel_out, keeps)
        rows = slice(row * C, row * C + C)
        pair = latent_ref[row // 2 * 16 : row // 2 * 16 + 16, :].astype(F32)
        state = pair[row % 2 * C : row % 2 * C + C]
        inc_ref[rows, :] = (drift[0] * state + fresh_ref[rows, :] + eps[0] * pred).astype(inc_ref.dtype)

    for beat in range(H // 2 + 4):
        if beat < H // 2:
            load(beat)
        if 0 <= beat - 2 < H // 2:
            widen(2 * (beat - 2))
            widen(2 * (beat - 2) + 1)
        if 0 <= beat - 4:
            narrow(2 * (beat - 4))
            narrow(2 * (beat - 4) + 1)


def scan_kernel(inclusive, x_ref, start_ref, out_ref):
    total = start_ref[...]
    for pair in range(16):
        rows = slice(pair * 16, pair * 16 + 16)
        both = x_ref[rows, :].astype(F32)
        middle = total + both[:C]
        after = middle + both[C:]
        kept = [middle, after] if inclusive else [total, middle]
        out_ref[rows, :] = jnp.concatenate(kept, axis=0).astype(out_ref.dtype)
        total = after


def final_kernel(state_ref, out_ref):
    for plane, block, rows, lanes in tiles():
        out_ref[:, plane, block * 8 : block * 8 + 8, :] = jnp.swapaxes(state_ref[rows, lanes].reshape(8, C, W), 0, 1)


VMEM = pl.BlockSpec(memory_space=pltpu.VMEM)
SMEM = pl.BlockSpec(memory_space=pltpu.SMEM)


def near(array):
    return pltpu.with_memory_space_constraint(array, pltpu.VMEM)


def call(kernel, scalars, arrays, outs, scratch=(), name=None):
    return pl.pallas_call(
        kernel,
        out_shape=outs if len(outs) > 1 else outs[0],
        in_specs=[SMEM] * len(scalars) + [VMEM] * len(arrays),
        out_specs=[VMEM] * len(outs) if len(outs) > 1 else VMEM,
        scratch_shapes=scratch,
        name=name,
    )(*scalars, *arrays)


def on_device(trajectory, first_latent, noise_draw, w_in, bias_in, level_bias, w_out, bias_out, drift, eps, scale):
    slabs = lax.axis_size("slab")
    levels = lax.axis_size("level")
    pairs = [(i, i ^ 1) for i in range(slabs)]
    crossings = [(i, j) for k in range(1, slabs - 1, 2) for i, j in ((k, k + 1), (k + 1, k))]

    latent = call(latent_kernel, (), (trajectory[0],), [pltpu.VMEM(ROWS, BF)], name="latent")
    fresh, start, kernel_in, kernel_out = call(
        prepare_kernel,
        (eps, scale),
        (
            noise_draw[0], first_latent,
            jnp.transpose(w_in, (2, 3, 4, 1, 0)).reshape(27, C, HID), bias_in[None], level_bias,
            jnp.transpose(w_out, (2, 3, 4, 0, 1)).reshape(27, C, HID), bias_out[None],
        ),
        [pltpu.VMEM(ROWS, F32), pltpu.VMEM((C, 2 * W), F32), pltpu.VMEM((HID, 240), BF), pltpu.VMEM((72, 3 * HID), BF)],
        [pltpu.VMEM(ROWS, F32)],
        name="prepare",
    )

    def step(latent, sent):
        crossed = lax.ppermute(latent, "slab", crossings)
        paired = lax.ppermute(latent, "slab", pairs)
        inc = call(
            lambda *refs: step_kernel(slabs, *refs),
            (drift, eps),
            [near(a) for a in (paired, latent, crossed, kernel_in, kernel_out, fresh)],
            [pltpu.VMEM(ROWS, sent)],
            [pltpu.VMEM((H + 2, 80, 4 * W), BF), pltpu.VMEM((H + 2, HID, 4 * W), BF)],
            name="step",
        )
        return exchange(inc)

    def exchange(array):
        return lax.all_to_all(array.reshape(levels, -1, 2 * W), "level", 0, 0).reshape(ROWS)

    def scan(inc, inclusive, kept):
        out = call(
            lambda *refs: scan_kernel(inclusive, *refs), (), [near(inc), near(start)], [pltpu.VMEM(ROWS, kept)], name="scan"
        )
        return exchange(out)

    latent = scan(step(latent, F32), False, BF)
    state = scan(step(latent, BF), True, F32)
    return call(final_kernel, (), (near(state),), [jax.ShapeDtypeStruct((C, 2, H, W), F32)], name="final")[None]


def solution(mesh):
    placed = (
        P("level", None, "slab", None, None),
        P(None, "slab", None, None),
        P("level", None, "slab", None, None),
        P(),
        P(),
        P("level", None),
        P(),
        P(),
        P("level"),
        P("level"),
        P("level"),
    )
    return jax.shard_map(
        on_device,
        mesh=mesh,
        in_specs=placed,
        out_specs=P("level", None, "slab", None, None),
        check_vma=False,
    )
```

```python
import jax
import jax.numpy as jnp
from jax import lax
from jax.experimental import pallas as pl
from jax.experimental.pallas import tpu as pltpu
from jax.sharding import PartitionSpec as P

C, HID, H, W = 8, 64, 32, 128
BF, F32 = jnp.bfloat16, jnp.float32
GROUP = 8
OWN = H // GROUP
EXT = OWN + 4
LANES = 2 * W
KEEP, EDGE = OWN * C, EXT * C
MESSAGE = EDGE + 2 * KEEP + 16
TAPS = 9 * C + C


def swapped(ref, plane, block):
    tile = ref[:, plane, block * 8 : block * 8 + 8, :]
    return jnp.swapaxes(tile, 0, 1).reshape(64, W)


def tiles():
    for plane in range(2):
        for block in range(4):
            yield plane, block, slice(block * 64, block * 64 + 64), slice(plane * W, plane * W + W)


def split(value, parts):
    pieces = []
    for _ in range(parts):
        pieces.append(value.astype(BF).astype(F32))
        value = value - pieces[-1]
    return pieces


def latent_kernel(x_ref, out_ref):
    for plane, block, rows, lanes in tiles():
        out_ref[rows, lanes] = swapped(x_ref, plane, block).astype(BF)


def stacked_kernel(pieces, pads):
    rows = []
    for kh in range(3):
        rows += pieces[kh] + [pads[kh]]
    return jnp.concatenate(rows, axis=0)


def turned(stacked):
    spare = jnp.zeros((256 - 3 * TAPS, W), F32)
    return jnp.concatenate([stacked, spare], axis=0).T[:HID, : 3 * TAPS].astype(BF)


def prepare_kernel(
    drift, eps, scale, noise_ref, first_ref, w_in_ref, bias_in_ref, level_bias_ref, w_out_ref, bias_out_ref,
    fresh_ref, start_ref, kernel_in_ref, spread_ref, kernel_out_ref, params_ref, first,
):
    same = lax.broadcasted_iota(jnp.int32, (C, C), 0) == lax.broadcasted_iota(jnp.int32, (C, C), 1)
    column = jnp.sum(jnp.where(same, jnp.broadcast_to(bias_out_ref[...], (C, C)), 0.0), axis=1, keepdims=True)
    shift = jnp.concatenate([jnp.broadcast_to(eps[0] * column, (C, W))] * 8, axis=0)
    edge = jnp.zeros((2 * C, LANES), F32)
    first[: 2 * C, :] = edge
    first[2 * C + H * C :, :] = edge
    for plane, block, rows, lanes in tiles():
        fresh_ref[rows, lanes] = scale[0] * swapped(noise_ref, plane, block) + shift
        first[rows.start + 2 * C : rows.stop + 2 * C, lanes] = swapped(first_ref, plane, block)
    own = pl.multiple_of(lax.axis_index("level") % GROUP * KEEP, KEEP)
    start_ref[...] = first[pl.ds(own, EDGE), :]

    bias = 0.5 * (bias_in_ref[...] + level_bias_ref[...])
    bias = jnp.concatenate([bias, jnp.zeros((1, LANES - HID), F32)], axis=1)
    rows = split(bias, 3)
    for scalar in (drift, eps):
        rows += split(jnp.full((1, LANES), scalar[0], F32), 3)
    index = lax.broadcasted_iota(jnp.int32, (16, LANES), 0)
    params = jnp.zeros((16, LANES), F32)
    for k, row in enumerate(rows):
        params = jnp.where(index == k, row, params)
    params_ref[...] = params.astype(BF)

    wide = jnp.zeros((C, W - HID), F32)
    pieces = [
        [
            jnp.concatenate([0.5 * w_in_ref[kd * 9 + kh * 3 + kw].astype(F32), wide], axis=1)
            for kd in range(3)
            for kw in range(3)
        ]
        for kh in range(3)
    ]
    nothing = jnp.zeros((C, W), F32)
    top = lax.broadcasted_iota(jnp.int32, (C, W), 0) == 0
    spread_ref[...] = stacked_kernel(pieces, [nothing] * 3)
    kernel_in_ref[...] = turned(stacked_kernel(pieces, [jnp.where(top, rows[kh][:, :W], 0.0) for kh in range(3)]))
    rows_of = [
        jnp.concatenate([w_out_ref[kd * 9 + kh * 3 + kw].astype(F32) for kd in range(3) for kw in range(3)], axis=0)
        for kh in range(3)
    ]
    kernel_out_ref[...] = jnp.concatenate(rows_of, axis=1).astype(BF)


def edge_masks():
    lane = lax.broadcasted_iota(jnp.int32, (C, W), 1)
    return lane > 0, lane < W - 1


def from_left(tile, keep):
    return jnp.where(keep, pltpu.roll(tile, 1, 1), 0.0)


def from_right(tile, keep):
    return jnp.where(keep, pltpu.roll(tile, W - 1, 1), 0.0)


def selector(slot):
    return jnp.where(lax.broadcasted_iota(jnp.int32, (C, 4 * W), 0) == slot, 1.0, 0.0).astype(F32)


def taps_of(row, keeps, chosen):
    blocks = [row[:, p * W : p * W + W] for p in range(6)]
    shifted = (
        [from_left(b, keeps[0]) for b in blocks],
        blocks,
        [from_right(b, keeps[1]) for b in blocks],
    )
    pieces = [jnp.concatenate(shifted[kw][kd : kd + 4], axis=1) for kd in range(3) for kw in range(3)]
    return jnp.concatenate(pieces + [chosen], axis=0).astype(BF)


def hidden_of(taps, kernel_in, inside, exists=None):
    u = jnp.dot(kernel_in, taps, preferred_element_type=F32)
    left, middle, right = u[:, :W] * inside[0], u[:, W : 3 * W], u[:, 3 * W :] * inside[1]
    u = jnp.concatenate([left, middle, right], axis=1)
    if exists is not None:
        u = u * exists
    return (u + u * jnp.tanh(u)).astype(BF)


def predicted_of(hidden, kernel_out, keeps):
    y = jnp.dot(kernel_out, hidden, preferred_element_type=F32)
    planes = []
    for plane in range(2):
        sums = []
        for kw in range(3):
            parts = [
                y[(kd * 3 + kw) * C : (kd * 3 + kw) * C + C, (plane + kd) * W : (plane + kd) * W + W]
                for kd in range(3)
            ]
            sums.append(parts[0] + parts[1] + parts[2])
        planes.append(sums[1] + from_left(sums[0], keeps[0]) + from_right(sums[2], keeps[1]))
    return jnp.concatenate(planes, axis=1)


def one_if(condition):
    return jnp.where(condition, 1.0, 0.0).astype(F32)


def slab_facts(slabs):
    slab = lax.axis_index("slab")
    return slab % 2 == 1, (one_if(slab > 0), one_if(slab < slabs - 1))


def six_planes(rows, odd, paired_ref, latent_ref, crossed_ref):
    paired, crossed = paired_ref[rows, :].astype(F32), crossed_ref[rows, :].astype(F32)
    below, above = jnp.where(odd, paired, crossed), jnp.where(odd, crossed, paired)
    return jnp.concatenate([below, latent_ref[rows, :].astype(F32), above], axis=1)


def first_step_kernel(
    slabs, drift, eps, paired_ref, latent_ref, crossed_ref, kernel_in_ref, kernel_out_ref, fresh_ref, params_ref,
    out_ref, taps, hidden,
):
    keeps = edge_masks()
    odd, inside = slab_facts(slabs)
    kernel_in, kernel_out = kernel_in_ref[...], kernel_out_ref[...]
    chosen = selector(0)
    empty = jnp.concatenate([jnp.zeros((9 * C, 4 * W), F32), chosen], axis=0).astype(BF)
    for edge in (0, H + 1):
        taps[edge] = empty
        hidden[edge] = jnp.zeros((HID, 4 * W), BF)
    out_ref[: 2 * C, :] = jnp.zeros((2 * C, LANES), BF)
    last = (GROUP - 1) * MESSAGE + EDGE
    out_ref[last - 2 * C : last, :] = jnp.zeros((2 * C, LANES), BF)
    for peer in range(GROUP):
        out_ref[(peer + 1) * MESSAGE - 16 : (peer + 1) * MESSAGE, :] = params_ref[...]

    def load(pair):
        both = six_planes(slice(pair * 16, pair * 16 + 16), odd, paired_ref, latent_ref, crossed_ref)
        for k in range(2):
            taps[1 + pair * 2 + k] = taps_of(both[k * C : k * C + C], keeps, chosen)

    def widen(row):
        hidden[1 + row] = hidden_of(taps[row : row + 3].reshape(3 * TAPS, 4 * W), kernel_in, inside)

    def narrow(pair):
        preds = [
            predicted_of(hidden[row : row + 3].reshape(3 * HID, 4 * W), kernel_out, keeps)
            for row in (2 * pair, 2 * pair + 1)
        ]
        rows = slice(pair * 16, pair * 16 + 16)
        fresh = fresh_ref[rows, :]
        inc = drift[0] * latent_ref[rows, :].astype(F32) + fresh + eps[0] * jnp.concatenate(preds, axis=0)
        high = inc.astype(BF)
        for peer in range(GROUP):
            at = 2 * pair - (OWN * peer - 2)
            if 0 <= at < EXT:
                base = peer * MESSAGE + at * C
                out_ref[base : base + 16, :] = high
        peer = 2 * pair // OWN
        base = peer * MESSAGE + EDGE + (2 * pair - OWN * peer) * C
        out_ref[base : base + 16, :] = (inc - high.astype(F32)).astype(BF)
        out_ref[base + KEEP : base + KEEP + 16, :] = fresh.astype(BF)

    for beat in range(H // 2 + 4):
        if beat < H // 2:
            load(beat)
        if 0 <= beat - 2 < H // 2:
            widen(2 * (beat - 2))
            widen(2 * (beat - 2) + 1)
        if 0 <= beat - 4:
            narrow(beat - 4)


def scan_kernel(x_ref, before_ref, total_ref):
    for block in range(EXT // 2):
        at = block * 16
        low = at - 2 * C
        total = jnp.zeros((16, LANES), F32)
        for k in range(GROUP):
            before_ref[k * EDGE + at : k * EDGE + at + 16, :] = total
            base = k * MESSAGE
            total = total + x_ref[base + at : base + at + 16, :].astype(F32)
            if 0 <= low < KEEP:
                total = total + x_ref[base + EDGE + low : base + EDGE + low + 16, :].astype(F32)
        high = total.astype(BF)
        total_ref[at : at + 16, :] = high
        if 0 <= low < KEEP:
            total_ref[EDGE + low : EDGE + low + 16, :] = (total - high.astype(F32)).astype(BF)


def tune_kernel(x_ref, spread_ref, kernel_in_ref, coefs_ref):
    params = [x_ref[(k + 1) * MESSAGE - 16 : (k + 1) * MESSAGE, :].astype(F32) for k in range(GROUP)]
    index = lax.broadcasted_iota(jnp.int32, (GROUP, LANES), 0)

    def gathered(row):
        out = jnp.zeros((GROUP, LANES), F32)
        for k in range(GROUP):
            out = jnp.where(index == k, params[k][row : row + 1], out)
        return out

    pieces = [
        [spread_ref[kh * TAPS + k * C : kh * TAPS + k * C + C, :] for k in range(9)] for kh in range(3)
    ]
    kernel_in_ref[...] = turned(stacked_kernel(pieces, [gathered(kh)[:, :W] for kh in range(3)]))
    coefs_ref[:GROUP, :] = gathered(3) + gathered(4) + gathered(5)
    coefs_ref[GROUP:, :] = gathered(6) + gathered(7) + gathered(8)


def state_kernel(start_ref, one_ref, two_ref, three_ref, before_ref, latent_ref):
    for block in range(EXT // 2):
        rows = slice(block * 16, block * 16 + 16)
        offset = start_ref[rows, :]
        for ref in (one_ref, two_ref, three_ref):
            offset = offset + ref[rows, :].astype(F32)
            if 2 * C <= rows.start < 2 * C + KEEP:
                offset = offset + ref[rows.start + EDGE - 2 * C : rows.stop + EDGE - 2 * C, :].astype(F32)
        for k in range(GROUP):
            at = slice(k * EDGE + rows.start, k * EDGE + rows.stop)
            latent_ref[at, :] = (offset + before_ref[at, :]).astype(BF)


def second_step_kernel(
    slabs, paired_ref, latent_ref, crossed_ref, kernel_in_ref, kernel_out_ref, x_ref, coefs_ref,
    sum_ref, total_ref, taps, hidden,
):
    keeps = edge_masks()
    odd, inside = slab_facts(slabs)
    part = lax.axis_index("level") % GROUP
    exists = {0: one_if(part > 0), EXT - 3: one_if(part < GROUP - 1)}
    kernel_in, kernel_out = kernel_in_ref[...], kernel_out_ref[...]
    chosen = [selector(k) for k in range(GROUP)]
    running = [jnp.zeros((16, LANES), F32) for _ in range(OWN // 2)]

    def load(level, pair):
        at = level * EDGE + pair * 16
        both = six_planes(slice(at, at + 16), odd, paired_ref, latent_ref, crossed_ref)
        for k in range(2):
            taps[level * EXT + pair * 2 + k] = taps_of(both[k * C : k * C + C], keeps, chosen[level])

    def widen(level, row):
        at = level * EXT + row
        hidden[level * (EXT - 2) + row] = hidden_of(
            taps[at : at + 3].reshape(3 * TAPS, 4 * W), kernel_in, inside, exists.get(row)
        )

    def narrow(level, pair):
        at = level * (EXT - 2) + 2 * pair
        preds = [
            predicted_of(hidden[row : row + 3].reshape(3 * HID, 4 * W), kernel_out, keeps) for row in (at, at + 1)
        ]
        base = level * EDGE + 2 * C + pair * 16
        fresh = level * MESSAGE + EDGE + KEEP + pair * 16
        inc = coefs_ref[level : level + 1, :] * latent_ref[base : base + 16, :].astype(F32)
        inc = inc + x_ref[fresh : fresh + 16, :].astype(F32)
        inc = inc + coefs_ref[GROUP + level : GROUP + level + 1, :] * jnp.concatenate(preds, axis=0)
        running[pair] = running[pair] + inc
        sum_ref[level * KEEP + pair * 16 : level * KEEP + pair * 16 + 16, :] = running[pair]
        if level == GROUP - 1:
            total_ref[pair * 16 : pair * 16 + 16, :] = running[pair]

    for beat in range(GROUP + 2):
        loads = [(load, beat, k) for k in range(EXT // 2)] if beat < GROUP else []
        widens = [(widen, beat - 1, k) for k in range(EXT - 2)] if 0 <= beat - 1 < GROUP else []
        narrows = [(narrow, beat - 2, k) for k in range(OWN // 2)] if 0 <= beat - 2 else []
        jobs = [((k + 0.5) / len(each), job) for each in (loads, widens, narrows) for k, job in enumerate(each)]
        for _, (work, *where) in sorted(jobs, key=lambda job: job[0]):
            work(*where)


def add_kernel(start_ref, one_ref, two_ref, three_ref, sum_ref, out_ref):
    offset = start_ref[2 * C : 2 * C + KEEP, :] + (one_ref[...] + two_ref[...] + three_ref[...])
    for k in range(GROUP):
        rows = slice(k * KEEP, k * KEEP + KEEP)
        out_ref[rows, :] = offset + sum_ref[rows, :]


def final_kernel(state_ref, out_ref):
    for plane, block, rows, lanes in tiles():
        out_ref[:, plane, block * 8 : block * 8 + 8, :] = jnp.swapaxes(state_ref[rows, lanes].reshape(8, C, W), 0, 1)


VMEM = pl.BlockSpec(memory_space=pltpu.VMEM)
SMEM = pl.BlockSpec(memory_space=pltpu.SMEM)


def near(*arrays):
    return [pltpu.with_memory_space_constraint(array, pltpu.VMEM) for array in arrays]


def call(kernel, scalars, arrays, outs, scratch=(), name=None):
    return pl.pallas_call(
        kernel,
        out_shape=outs if len(outs) > 1 else outs[0],
        in_specs=[SMEM] * len(scalars) + [VMEM] * len(arrays),
        out_specs=[VMEM] * len(outs) if len(outs) > 1 else VMEM,
        scratch_shapes=scratch,
        name=name,
    )(*scalars, *arrays)


def on_device(trajectory, first_latent, noise_draw, w_in, bias_in, level_bias, w_out, bias_out, drift, eps, scale):
    slabs = lax.axis_size("slab")
    levels = lax.axis_size("level")
    pairs = [(i, i ^ 1) for i in range(slabs)]
    crossings = [(i, j) for k in range(1, slabs - 1, 2) for i, j in ((k, k + 1), (k + 1, k))]
    groups = [list(range(k, k + GROUP)) for k in range(0, levels, GROUP)]

    def neighbours(latent):
        crossed = lax.ppermute(latent, "slab", crossings)
        return lax.ppermute(latent, "slab", pairs), latent, crossed

    def exchange(array):
        parts = array.reshape(GROUP, -1, LANES)
        return lax.all_to_all(parts, "level", 0, 0, axis_index_groups=groups).reshape(array.shape)

    def earlier_groups(total):
        return [
            lax.ppermute(total, "level", [(i, i + k) for i in range(levels - k)]) for k in range(GROUP, levels, GROUP)
        ]

    latent = call(latent_kernel, (), (trajectory[0],), [pltpu.VMEM((H * C, LANES), BF)], name="latent")
    fresh, start, kernel_in, spread, kernel_out, params = call(
        prepare_kernel,
        (drift, eps, scale),
        (
            noise_draw[0], first_latent,
            jnp.transpose(w_in, (2, 3, 4, 1, 0)).reshape(27, C, HID), bias_in[None], level_bias,
            jnp.transpose(w_out, (2, 3, 4, 0, 1)).reshape(27, C, HID), bias_out[None],
        ),
        [
            pltpu.VMEM((H * C, LANES), F32), pltpu.VMEM((EDGE, LANES), F32), pltpu.VMEM((HID, 3 * TAPS), BF),
            pltpu.VMEM((3 * TAPS, W), F32), pltpu.VMEM((9 * C, 3 * HID), BF), pltpu.VMEM((16, LANES), BF),
        ],
        [pltpu.VMEM(((H + 4) * C, LANES), F32)],
        name="prepare",
    )
    sent = call(
        lambda *refs: first_step_kernel(slabs, *refs),
        (drift, eps),
        near(*neighbours(latent), kernel_in, kernel_out, fresh, params),
        [pltpu.VMEM((GROUP * MESSAGE, LANES), BF)],
        [pltpu.VMEM((H + 2, TAPS, 4 * W), BF), pltpu.VMEM((H + 2, HID, 4 * W), BF)],
        name="first",
    )
    got = exchange(sent)
    before, total = call(
        scan_kernel, (), near(got),
        [pltpu.VMEM((GROUP * EDGE, LANES), F32), pltpu.VMEM((EDGE + KEEP, LANES), BF)], name="scan",
    )
    kernel_in, coefs = call(
        tune_kernel, (), near(got, spread),
        [pltpu.VMEM((HID, 3 * TAPS), BF), pltpu.VMEM((2 * GROUP, LANES), F32)], name="tune",
    )
    latent = call(
        state_kernel, (), near(start, *earlier_groups(total), before),
        [pltpu.VMEM((GROUP * EDGE, LANES), BF)], name="state",
    )
    sums, total = call(
        lambda *refs: second_step_kernel(slabs, *refs),
        (),
        near(*neighbours(latent), kernel_in, kernel_out, got, coefs),
        [pltpu.VMEM((GROUP * KEEP, LANES), F32), pltpu.VMEM((KEEP, LANES), F32)],
        [
            pltpu.VMEM((GROUP * EXT, TAPS, 4 * W), BF),
            pltpu.VMEM((GROUP * (EXT - 2), HID, 4 * W), BF),
        ],
        name="second",
    )
    state = call(
        add_kernel, (), near(start, *earlier_groups(total), sums), [pltpu.VMEM((GROUP * KEEP, LANES), F32)], name="add"
    )
    return call(
        final_kernel, (), near(exchange(state)), [jax.ShapeDtypeStruct((C, 2, H, W), F32)], name="final"
    )[None]


def solution(mesh):
    placed = (
        P("level", None, "slab", None, None),
        P(None, "slab", None, None),
        P("level", None, "slab", None, None),
        P(),
        P(),
        P("level", None),
        P(),
        P(),
        P("level"),
        P("level"),
        P("level"),
    )
    return jax.shard_map(
        on_device,
        mesh=mesh,
        in_specs=placed,
        out_specs=P("level", None, "slab", None, None),
        check_vma=False,
    )
```

```python
import jax
import jax.numpy as jnp
from jax import lax
from jax.experimental import pallas as pl
from jax.experimental.pallas import tpu as pltpu
from jax.sharding import PartitionSpec as P

C, HID, H, W = 8, 64, 32, 128
BF, F32 = jnp.bfloat16, jnp.float32
GROUP = 8
OWN = H // GROUP
EXT = OWN + 4
LANES = 2 * W
KEEP, EDGE = OWN * C, EXT * C
MESSAGE = EDGE + KEEP + C
TAPS = 9 * C + C


def swapped(ref, plane, block):
    tile = ref[:, plane, block * 8 : block * 8 + 8, :]
    return jnp.swapaxes(tile, 0, 1).reshape(64, W)


def tiles():
    for plane in range(2):
        for block in range(4):
            yield plane, block, slice(block * 64, block * 64 + 64), slice(plane * W, plane * W + W)


def split(value, parts):
    pieces = []
    for _ in range(parts):
        pieces.append(value.astype(BF).astype(F32))
        value = value - pieces[-1]
    return pieces


def latent_kernel(x_ref, out_ref):
    for plane, block, rows, lanes in tiles():
        out_ref[rows, lanes] = swapped(x_ref, plane, block).astype(BF)


def stacked_kernel(pieces, pads):
    rows = []
    for kh in range(3):
        rows += pieces[kh] + [pads[kh]]
    return jnp.concatenate(rows, axis=0)


def turned(stacked):
    spare = jnp.zeros((256 - 3 * TAPS, W), F32)
    return jnp.concatenate([stacked, spare], axis=0).T[:HID, : 3 * TAPS].astype(BF)


def prepare_kernel(
    drift_ref, eps_ref, scale_ref, x_ref, noise_ref, first_ref, w_in_ref, bias_in_ref, level_bias_ref, w_out_ref, bias_out_ref,
    base_ref, fresh_ref, start_ref, kernel_in_ref, spread_ref, kernel_out_ref, params_ref, first,
):
    same = lax.broadcasted_iota(jnp.int32, (C, C), 0) == lax.broadcasted_iota(jnp.int32, (C, C), 1)
    drift, eps, scale = (jnp.full((1, W), ref[0], F32) for ref in (drift_ref, eps_ref, scale_ref))
    column = jnp.sum(jnp.where(same, jnp.broadcast_to(bias_out_ref[...], (C, C)), 0.0), axis=1, keepdims=True)
    shift = jnp.concatenate([eps * jnp.broadcast_to(column, (C, W))] * 8, axis=0)
    edge = jnp.zeros((2 * C, LANES), F32)
    first[: 2 * C, :] = edge
    first[2 * C + H * C :, :] = edge
    for plane, block, rows, lanes in tiles():
        fresh = scale * swapped(noise_ref, plane, block) + shift
        fresh_ref[rows, lanes] = fresh
        base_ref[rows, lanes] = drift * swapped(x_ref, plane, block) + fresh
        first[rows.start + 2 * C : rows.stop + 2 * C, lanes] = swapped(first_ref, plane, block)
    own = pl.multiple_of(lax.axis_index("level") % GROUP * KEEP, KEEP)
    start_ref[...] = first[pl.ds(own, EDGE), :]

    bias = 0.5 * (bias_in_ref[...] + level_bias_ref[...])
    bias = jnp.concatenate([bias, jnp.zeros((1, W - HID), F32)], axis=1)
    rows = split(bias, 3)
    index = lax.broadcasted_iota(jnp.int32, (C, W), 0)
    left = right = jnp.zeros((C, W), F32)
    for k, row in enumerate(rows + split(drift, 3)):
        left = jnp.where(index == k, row, left)
    for k, row in enumerate(split(eps, 3)):
        right = jnp.where(index == 3 + k, row, right)
    params_ref[...] = jnp.concatenate([left, right], axis=1).astype(BF)

    wide = jnp.zeros((C, W - HID), F32)
    pieces = [
        [
            jnp.concatenate([0.5 * w_in_ref[kd * 9 + kh * 3 + kw].astype(F32), wide], axis=1)
            for kd in range(3)
            for kw in range(3)
        ]
        for kh in range(3)
    ]
    nothing = jnp.zeros((C, W), F32)
    top = lax.broadcasted_iota(jnp.int32, (C, W), 0) == 0
    spread_ref[...] = stacked_kernel(pieces, [nothing] * 3)
    kernel_in_ref[...] = turned(stacked_kernel(pieces, [jnp.where(top, rows[kh], 0.0) for kh in range(3)]))
    rows_of = [
        jnp.concatenate([w_out_ref[kd * 9 + kh * 3 + kw].astype(F32) for kd in range(3) for kw in range(3)], axis=0)
        for kh in range(3)
    ]
    kernel_out_ref[...] = jnp.concatenate(rows_of, axis=1).astype(BF)


def edge_masks():
    lane = lax.broadcasted_iota(jnp.int32, (C, W), 1)
    return lane > 0, lane < W - 1


def from_left(tile, keep):
    return jnp.where(keep, pltpu.roll(tile, 1, 1), 0.0)


def from_right(tile, keep):
    return jnp.where(keep, pltpu.roll(tile, W - 1, 1), 0.0)


def selector(slot):
    return jnp.where(lax.broadcasted_iota(jnp.int32, (C, 4 * W), 0) == slot, 1.0, 0.0).astype(F32)


def taps_of(row, keeps, chosen):
    blocks = [row[:, p * W : p * W + W] for p in range(6)]
    shifted = (
        [from_left(b, keeps[0]) for b in blocks],
        blocks,
        [from_right(b, keeps[1]) for b in blocks],
    )
    pieces = [jnp.concatenate(shifted[kw][kd : kd + 4], axis=1) for kd in range(3) for kw in range(3)]
    return jnp.concatenate(pieces + [chosen], axis=0).astype(BF)


def hidden_of(taps, kernel_in, inside, exists=None):
    u = jnp.dot(kernel_in, taps, preferred_element_type=F32)
    out = (u + u * jnp.tanh(u)).astype(BF)
    if exists is not None:
        out = out * jnp.concatenate([exists] * 4, axis=1)
    return jnp.concatenate([out[:, :W] * inside[0], out[:, W : 3 * W], out[:, 3 * W :] * inside[1]], axis=1)


def predicted_of(hidden, kernel_out, keeps):
    y = jnp.dot(kernel_out, hidden, preferred_element_type=F32)
    planes = []
    for plane in range(2):
        sums = []
        for kw in range(3):
            parts = [
                y[(kd * 3 + kw) * C : (kd * 3 + kw) * C + C, (plane + kd) * W : (plane + kd) * W + W]
                for kd in range(3)
            ]
            sums.append(parts[0] + parts[1] + parts[2])
        planes.append(sums[1] + from_left(sums[0], keeps[0]) + from_right(sums[2], keeps[1]))
    return jnp.concatenate(planes, axis=1)


def one_if(condition):
    return jnp.broadcast_to(jnp.where(condition, 1.0, 0.0).astype(F32), (1, W)).astype(BF)


def slab_facts(slabs):
    slab = lax.axis_index("slab")
    return slab % 2 == 1, (one_if(slab > 0), one_if(slab < slabs - 1))


def six_planes(odd, paired, own, crossed):
    below, above = jnp.where(odd, paired, crossed), jnp.where(odd, crossed, paired)
    return jnp.concatenate([below, own, above], axis=1)


def first_step_kernel(
    slabs, paired_ref, latent_ref, crossed_ref, kernel_in_ref, kernel_out_ref, base_ref, fresh_ref, params_ref,
    out_ref, taps, hidden,
):
    keeps = edge_masks()
    odd, inside = slab_facts(slabs)
    kernel_in, kernel_out = kernel_in_ref[...], kernel_out_ref[...]
    eps = sum(params_ref[...].astype(F32)[row : row + 1, W:] for row in (3, 4, 5))
    eps = jnp.concatenate([eps, eps], axis=1)
    chosen = selector(0)
    empty = jnp.concatenate([jnp.zeros((9 * C, 4 * W), F32), chosen], axis=0).astype(BF)
    for edge in (0, H + 1):
        taps[edge] = empty
        hidden[edge] = jnp.zeros((HID, 4 * W), BF)
    out_ref[: 2 * C, :] = jnp.zeros((2 * C, LANES), BF)
    last = (GROUP - 1) * MESSAGE + EDGE
    out_ref[last - 2 * C : last, :] = jnp.zeros((2 * C, LANES), BF)
    for peer in range(GROUP):
        out_ref[(peer + 1) * MESSAGE - C : (peer + 1) * MESSAGE, :] = params_ref[...]

    def load(pair):
        rows = slice(pair * 16, pair * 16 + 16)
        both = six_planes(odd, *[ref[rows, :].astype(F32) for ref in (paired_ref, latent_ref, crossed_ref)])
        for k in range(2):
            taps[1 + pair * 2 + k] = taps_of(both[k * C : k * C + C], keeps, chosen)

    def widen(row):
        hidden[1 + row] = hidden_of(taps[row : row + 3].reshape(3 * TAPS, 4 * W), kernel_in, inside)

    def narrow(pair):
        preds = [
            predicted_of(hidden[row : row + 3].reshape(3 * HID, 4 * W), kernel_out, keeps)
            for row in (2 * pair, 2 * pair + 1)
        ]
        rows = slice(pair * 16, pair * 16 + 16)
        inc = base_ref[rows, :] + eps * jnp.concatenate(preds, axis=0)
        known = (inc - fresh_ref[rows, :]).astype(BF)
        for peer in range(GROUP):
            at = 2 * pair - (OWN * peer - 2)
            if 0 <= at < EXT:
                base = peer * MESSAGE + at * C
                out_ref[base : base + 16, :] = known if 2 <= at < 2 + OWN else inc.astype(BF)
        peer = 2 * pair // OWN
        base = peer * MESSAGE + EDGE + (2 * pair - OWN * peer) * C
        out_ref[base : base + 16, :] = (inc - known.astype(F32)).astype(BF)

    for beat in range(H // 2 + 4):
        if beat < H // 2:
            load(beat)
        if 0 <= beat - 2 < H // 2:
            widen(2 * (beat - 2))
            widen(2 * (beat - 2) + 1)
        if 0 <= beat - 4:
            narrow(beat - 4)


def scan_kernel(x_ref, before_ref, total_ref):
    for block in range(EXT // 2):
        at = block * 16
        low = at - 2 * C
        total = jnp.zeros((16, LANES), F32)
        for k in range(GROUP):
            rows = slice(k * EDGE + at, k * EDGE + at + 16)
            before_ref[rows, :] = total
            base = k * MESSAGE
            total = total + x_ref[base + at : base + at + 16, :].astype(F32)
            if 0 <= low < KEEP:
                total = total + x_ref[base + EDGE + low : base + EDGE + low + 16, :].astype(F32)
        high = total.astype(BF)
        total_ref[at : at + 16, :] = high
        if 0 <= low < KEEP:
            total_ref[EDGE + low : EDGE + low + 16, :] = (total - high.astype(F32)).astype(BF)


def state_kernel(start_ref, one_ref, two_ref, three_ref, before_ref, state_ref, latent_ref):
    for block in range(EXT // 2):
        rows = slice(block * 16, block * 16 + 16)
        low = rows.start - 2 * C
        offset = start_ref[rows, :]
        for ref in (one_ref, two_ref, three_ref):
            offset = offset + ref[rows, :].astype(F32)
            if 0 <= low < KEEP:
                offset = offset + ref[EDGE + low : EDGE + low + 16, :].astype(F32)
        for k in range(GROUP):
            at = slice(k * EDGE + rows.start, k * EDGE + rows.stop)
            state = offset + before_ref[at, :]
            latent_ref[at, :] = state.astype(BF)
            if 0 <= low < KEEP:
                state_ref[k * KEEP + low : k * KEEP + low + 16, :] = state


def tune_kernel(x_ref, spread_ref, kernel_in_ref, coefs_ref):
    params = [x_ref[(k + 1) * MESSAGE - C : (k + 1) * MESSAGE, :].astype(F32) for k in range(GROUP)]
    index = lax.broadcasted_iota(jnp.int32, (GROUP, LANES), 0)

    def gathered(row):
        out = jnp.zeros((GROUP, LANES), F32)
        for k in range(GROUP):
            out = jnp.where(index == k, params[k][row : row + 1], out)
        return out

    pieces = [
        [spread_ref[kh * TAPS + k * C : kh * TAPS + k * C + C, :] for k in range(9)] for kh in range(3)
    ]
    kernel_in_ref[...] = turned(stacked_kernel(pieces, [gathered(kh)[:, :W] for kh in range(3)]))
    coefs = gathered(3) + gathered(4) + gathered(5)
    coefs_ref[:GROUP, :] = jnp.concatenate([coefs[:, :W]] * 2, axis=1)
    coefs_ref[GROUP:, :] = jnp.concatenate([coefs[:, W:]] * 2, axis=1)


def second_step_kernel(
    slabs, paired_ref, latent_ref, crossed_ref, kernel_in_ref, kernel_out_ref, x_ref, coefs_ref, state_ref,
    sum_ref, total_ref, taps, hidden,
):
    keeps = edge_masks()
    odd, inside = slab_facts(slabs)
    part = lax.axis_index("level") % GROUP
    exists = {0: one_if(part > 0), EXT - 3: one_if(part < GROUP - 1)}
    kernel_in, kernel_out = kernel_in_ref[...], kernel_out_ref[...]
    chosen = [selector(k) for k in range(GROUP)]
    running = [jnp.zeros((16, LANES), F32) for _ in range(OWN // 2)]

    def load(level, pair):
        at = level * EDGE + pair * 16
        refs = (paired_ref, latent_ref, crossed_ref)
        both = six_planes(odd, *[ref[at : at + 16, :].astype(F32) for ref in refs])
        for k in range(2):
            taps[level * EXT + pair * 2 + k] = taps_of(both[k * C : k * C + C], keeps, chosen[level])

    def widen(level, row):
        at = level * EXT + row
        hidden[level * (EXT - 2) + row] = hidden_of(
            taps[at : at + 3].reshape(3 * TAPS, 4 * W), kernel_in, inside, exists.get(row)
        )

    def narrow(level, pair):
        at = level * (EXT - 2) + 2 * pair
        preds = [
            predicted_of(hidden[row : row + 3].reshape(3 * HID, 4 * W), kernel_out, keeps) for row in (at, at + 1)
        ]
        base = level * KEEP + pair * 16
        fresh = level * MESSAGE + EDGE + pair * 16
        inc = coefs_ref[level : level + 1, :] * state_ref[base : base + 16, :]
        inc = inc + x_ref[fresh : fresh + 16, :].astype(F32)
        inc = inc + coefs_ref[GROUP + level : GROUP + level + 1, :] * jnp.concatenate(preds, axis=0)
        running[pair] = running[pair] + inc
        sum_ref[level * KEEP + pair * 16 : level * KEEP + pair * 16 + 16, :] = running[pair]
        if level == GROUP - 1:
            total_ref[pair * 16 : pair * 16 + 16, :] = running[pair]

    for beat in range(GROUP + 2):
        loads = [(load, beat, k) for k in range(EXT // 2)] if beat < GROUP else []
        widens = [(widen, beat - 1, k) for k in range(EXT - 2)] if 0 <= beat - 1 < GROUP else []
        narrows = [(narrow, beat - 2, k) for k in range(OWN // 2)] if 0 <= beat - 2 else []
        jobs = [((k + 0.5) / len(each), job) for each in (loads, widens, narrows) for k, job in enumerate(each)]
        for _, (work, *where) in sorted(jobs, key=lambda job: job[0]):
            work(*where)


def add_kernel(start_ref, one_ref, two_ref, three_ref, sum_ref, out_ref):
    offset = start_ref[2 * C : 2 * C + KEEP, :] + (one_ref[...] + two_ref[...] + three_ref[...])
    for k in range(GROUP):
        rows = slice(k * KEEP, k * KEEP + KEEP)
        out_ref[rows, :] = offset + sum_ref[rows, :]


def final_kernel(state_ref, out_ref):
    for plane, block, rows, lanes in tiles():
        out_ref[:, plane, block * 8 : block * 8 + 8, :] = jnp.swapaxes(state_ref[rows, lanes].reshape(8, C, W), 0, 1)


VMEM = pl.BlockSpec(memory_space=pltpu.VMEM)
SMEM = pl.BlockSpec(memory_space=pltpu.SMEM)


def near(*arrays):
    return [pltpu.with_memory_space_constraint(array, pltpu.VMEM) for array in arrays]


def call(kernel, arrays, outs, scratch=(), name=None, scalars=0):
    return pl.pallas_call(
        kernel,
        out_shape=outs if len(outs) > 1 else outs[0],
        in_specs=[SMEM] * scalars + [VMEM] * (len(arrays) - scalars),
        out_specs=[VMEM] * len(outs) if len(outs) > 1 else VMEM,
        scratch_shapes=scratch,
        name=name,
    )(*arrays)


def on_device(trajectory, first_latent, noise_draw, w_in, bias_in, level_bias, w_out, bias_out, drift, eps, scale):
    slabs = lax.axis_size("slab")
    levels = lax.axis_size("level")
    pairs = [(i, i ^ 1) for i in range(slabs)]
    crossings = [(i, j) for k in range(1, slabs - 1, 2) for i, j in ((k, k + 1), (k + 1, k))]
    groups = [list(range(k, k + GROUP)) for k in range(0, levels, GROUP)]

    def neighbours(latent):
        crossed = lax.ppermute(latent, "slab", crossings)
        return lax.ppermute(latent, "slab", pairs), latent, crossed

    def exchange(array):
        parts = array.reshape(GROUP, -1, LANES)
        return lax.all_to_all(parts, "level", 0, 0, axis_index_groups=groups).reshape(array.shape)

    def earlier_groups(total):
        return [
            lax.ppermute(total, "level", [(i, i + k) for i in range(levels - k)]) for k in range(GROUP, levels, GROUP)
        ]

    latent = call(latent_kernel, (trajectory[0],), [pltpu.VMEM((H * C, LANES), BF)], name="latent")
    base, fresh, start, kernel_in, spread, kernel_out, params = call(
        prepare_kernel,
        (
            drift, eps, scale,
            trajectory[0], noise_draw[0], first_latent,
            jnp.transpose(w_in, (2, 3, 4, 1, 0)).reshape(27, C, HID), bias_in[None], level_bias,
            jnp.transpose(w_out, (2, 3, 4, 0, 1)).reshape(27, C, HID), bias_out[None],
        ),
        [
            pltpu.VMEM((H * C, LANES), F32), pltpu.VMEM((H * C, LANES), F32), pltpu.VMEM((EDGE, LANES), F32),
            pltpu.VMEM((HID, 3 * TAPS), BF),
            pltpu.VMEM((3 * TAPS, W), F32), pltpu.VMEM((9 * C, 3 * HID), BF), pltpu.VMEM((C, LANES), BF),
        ],
        [pltpu.VMEM(((H + 4) * C, LANES), F32)],
        name="prepare",
        scalars=3,
    )
    sent = call(
        lambda *refs: first_step_kernel(slabs, *refs),
        near(*neighbours(latent), kernel_in, kernel_out, base, fresh, params),
        [pltpu.VMEM((GROUP * MESSAGE, LANES), BF)],
        [pltpu.VMEM((H + 2, TAPS, 4 * W), BF), pltpu.VMEM((H + 2, HID, 4 * W), BF)],
        name="first",
    )
    got = exchange(sent)
    before, total = call(
        scan_kernel, near(got),
        [pltpu.VMEM((GROUP * EDGE, LANES), F32), pltpu.VMEM((EDGE + KEEP, LANES), BF)], name="scan",
    )
    kernel_in, coefs = call(
        tune_kernel, near(got, spread),
        [pltpu.VMEM((HID, 3 * TAPS), BF), pltpu.VMEM((2 * GROUP, LANES), F32)], name="tune",
    )
    state, latent = call(
        state_kernel, near(start, *earlier_groups(total), before),
        [pltpu.VMEM((GROUP * KEEP, LANES), F32), pltpu.VMEM((GROUP * EDGE, LANES), BF)], name="state",
    )
    sums, total = call(
        lambda *refs: second_step_kernel(slabs, *refs),
        near(*neighbours(latent), kernel_in, kernel_out, got, coefs, state),
        [pltpu.VMEM((GROUP * KEEP, LANES), F32), pltpu.VMEM((KEEP, LANES), F32)],
        [
            pltpu.VMEM((GROUP * EXT, TAPS, 4 * W), BF),
            pltpu.VMEM((GROUP * (EXT - 2), HID, 4 * W), BF),
        ],
        name="second",
    )
    state = call(
        add_kernel, near(start, *earlier_groups(total), sums), [pltpu.VMEM((GROUP * KEEP, LANES), F32)], name="add"
    )
    return call(
        final_kernel, near(exchange(state)), [jax.ShapeDtypeStruct((C, 2, H, W), F32)], name="final"
    )[None]


def solution(mesh):
    placed = (
        P("level", None, "slab", None, None),
        P(None, "slab", None, None),
        P("level", None, "slab", None, None),
        P(),
        P(),
        P("level", None),
        P(),
        P(),
        P("level"),
        P("level"),
        P("level"),
    )
    return jax.shard_map(
        on_device,
        mesh=mesh,
        in_specs=placed,
        out_specs=P("level", None, "slab", None, None),
        check_vma=False,
    )
```

```python
import jax
import jax.numpy as jnp
from jax import lax
from jax.experimental import pallas as pl
from jax.experimental.pallas import tpu as pltpu
from jax.sharding import PartitionSpec as P

C, HID, H, W = 8, 64, 32, 128
BF, F32 = jnp.bfloat16, jnp.float32
GROUP = 8
OWN = H // GROUP
EXT = OWN + 4
LANES = 2 * W
KEEP, EDGE = OWN * C, EXT * C
MESSAGE = EDGE + KEEP + C
TAPS = 9 * C + C


def swapped(ref, plane, block):
    tile = ref[:, plane, block * 8 : block * 8 + 8, :]
    return jnp.swapaxes(tile, 0, 1).reshape(64, W)


def tiles():
    for plane in range(2):
        for block in range(4):
            yield plane, block, slice(block * 64, block * 64 + 64), slice(plane * W, plane * W + W)


def split(value, parts):
    pieces = []
    for _ in range(parts):
        pieces.append(value.astype(BF).astype(F32))
        value = value - pieces[-1]
    return pieces


def stacked_kernel(pieces, pads):
    rows = []
    for kh in range(3):
        rows += pieces[kh] + [pads[kh]]
    return jnp.concatenate(rows, axis=0)


def turned(stacked):
    spare = jnp.zeros((256 - 3 * TAPS, W), F32)
    return jnp.concatenate([stacked, spare], axis=0).T[:HID, : 3 * TAPS].astype(BF)


def opening_kernel(
    x_ref, noise_ref, first_ref, w_in_ref, bias_in_ref, level_bias_ref, w_out_ref, bias_out_ref,
    latent_ref, state_ref, noise_out_ref, start_ref, kernel_in_ref, spread_ref, kernel_out_ref, biases_ref, column_ref,
    first,
):
    edge = jnp.zeros((2 * C, LANES), F32)
    first[: 2 * C, :] = edge
    first[2 * C + H * C :, :] = edge
    for plane, block, rows, lanes in tiles():
        state = swapped(x_ref, plane, block)
        state_ref[rows, lanes] = state
        latent_ref[rows, lanes] = state.astype(BF)
        noise_out_ref[rows, lanes] = swapped(noise_ref, plane, block)
        first[rows.start + 2 * C : rows.stop + 2 * C, lanes] = swapped(first_ref, plane, block)
    own = pl.multiple_of(lax.axis_index("level") % GROUP * KEEP, KEEP)
    start_ref[...] = first[pl.ds(own, EDGE), :]

    same = lax.broadcasted_iota(jnp.int32, (C, C), 0) == lax.broadcasted_iota(jnp.int32, (C, C), 1)
    column = jnp.sum(jnp.where(same, jnp.broadcast_to(bias_out_ref[...], (C, C)), 0.0), axis=1, keepdims=True)
    column_ref[...] = jnp.broadcast_to(column, (C, W))
    bias = 0.5 * (bias_in_ref[...] + level_bias_ref[...])
    biases = split(jnp.concatenate([bias, jnp.zeros((1, W - HID), F32)], axis=1), 3)
    index = lax.broadcasted_iota(jnp.int32, (C, W), 0)
    nothing = jnp.zeros((C, W), F32)
    table = nothing
    for k, row in enumerate(biases):
        table = jnp.where(index == k, row, table)
    biases_ref[...] = table

    wide = jnp.zeros((C, W - HID), F32)
    pieces = [
        [
            jnp.concatenate([0.5 * w_in_ref[kd * 9 + kh * 3 + kw].astype(F32), wide], axis=1)
            for kd in range(3)
            for kw in range(3)
        ]
        for kh in range(3)
    ]
    spread_ref[...] = stacked_kernel(pieces, [nothing] * 3)
    kernel_in_ref[...] = turned(stacked_kernel(pieces, [jnp.where(index == 0, row, 0.0) for row in biases]))
    rows_of = [
        jnp.concatenate([w_out_ref[kd * 9 + kh * 3 + kw].astype(F32) for kd in range(3) for kw in range(3)], axis=0)
        for kh in range(3)
    ]
    kernel_out_ref[...] = jnp.concatenate(rows_of, axis=1).astype(BF)


def prepare_kernel(
    drift_ref, eps_ref, scale_ref, state_ref, noise_ref, biases_ref, column_ref, base_ref, fresh_ref, params_ref
):
    drift, eps, scale = (jnp.full((1, W), ref[0], F32) for ref in (drift_ref, eps_ref, scale_ref))
    column = eps * column_ref[...]
    shift = jnp.concatenate([column, column], axis=1)
    for row in range(H):
        rows = slice(row * C, row * C + C)
        fresh = scale_ref[0] * noise_ref[rows, :] + shift
        fresh_ref[rows, :] = fresh
        base_ref[rows, :] = drift_ref[0] * state_ref[rows, :] + fresh
    index = lax.broadcasted_iota(jnp.int32, (C, W), 0)
    left, right = biases_ref[...], jnp.zeros((C, W), F32)
    for k, row in enumerate(split(drift, 3)):
        left = jnp.where(index == 3 + k, row, left)
    for k, row in enumerate(split(eps, 3)):
        right = jnp.where(index == 3 + k, row, right)
    params_ref[...] = jnp.concatenate([left, right], axis=1).astype(BF)


def edge_masks():
    lane = lax.broadcasted_iota(jnp.int32, (C, W), 1)
    return lane > 0, lane < W - 1


def from_left(tile, keep):
    return jnp.where(keep, pltpu.roll(tile, 1, 1), 0.0)


def from_right(tile, keep):
    return jnp.where(keep, pltpu.roll(tile, W - 1, 1), 0.0)


def selector(slot):
    return jnp.where(lax.broadcasted_iota(jnp.int32, (C, 4 * W), 0) == slot, 1.0, 0.0).astype(F32)


def taps_of(row, keeps, chosen):
    blocks = [row[:, p * W : p * W + W] for p in range(6)]
    shifted = (
        [from_left(b, keeps[0]) for b in blocks],
        blocks,
        [from_right(b, keeps[1]) for b in blocks],
    )
    pieces = [jnp.concatenate(shifted[kw][kd : kd + 4], axis=1) for kd in range(3) for kw in range(3)]
    return jnp.concatenate(pieces + [chosen], axis=0).astype(BF)


def hidden_of(taps, kernel_in, inside, exists=None):
    u = jnp.dot(kernel_in, taps, preferred_element_type=F32)
    out = (u + u * jnp.tanh(u)).astype(BF)
    if exists is not None:
        out = out * jnp.concatenate([exists] * 4, axis=1)
    return jnp.concatenate([out[:, :W] * inside[0], out[:, W : 3 * W], out[:, 3 * W :] * inside[1]], axis=1)


def predicted_of(hidden, kernel_out, keeps):
    y = jnp.dot(kernel_out, hidden, preferred_element_type=F32)
    planes = []
    for plane in range(2):
        sums = []
        for kw in range(3):
            parts = [
                y[(kd * 3 + kw) * C : (kd * 3 + kw) * C + C, (plane + kd) * W : (plane + kd) * W + W]
                for kd in range(3)
            ]
            sums.append(parts[0] + parts[1] + parts[2])
        planes.append(sums[1] + from_left(sums[0], keeps[0]) + from_right(sums[2], keeps[1]))
    return jnp.concatenate(planes, axis=1)


def one_if(condition):
    return jnp.broadcast_to(jnp.where(condition, 1.0, 0.0).astype(F32), (1, W)).astype(BF)


def slab_facts(slabs):
    slab = lax.axis_index("slab")
    return slab % 2 == 1, (one_if(slab > 0), one_if(slab < slabs - 1))


def six_planes(odd, paired, own, crossed):
    below, above = jnp.where(odd, paired, crossed), jnp.where(odd, crossed, paired)
    return jnp.concatenate([below, own, above], axis=1)


def first_step_kernel(
    slabs, paired_ref, latent_ref, crossed_ref, kernel_in_ref, kernel_out_ref, base_ref, fresh_ref, params_ref,
    out_ref, taps, hidden,
):
    keeps = edge_masks()
    odd, inside = slab_facts(slabs)
    kernel_in, kernel_out = kernel_in_ref[...], kernel_out_ref[...]
    eps = sum(params_ref[...].astype(F32)[row : row + 1, W:] for row in (3, 4, 5))
    eps = jnp.concatenate([eps, eps], axis=1)
    chosen = selector(0)
    empty = jnp.concatenate([jnp.zeros((9 * C, 4 * W), F32), chosen], axis=0).astype(BF)
    for edge in (0, H + 1):
        taps[edge] = empty
        hidden[edge] = jnp.zeros((HID, 4 * W), BF)
    out_ref[: 2 * C, :] = jnp.zeros((2 * C, LANES), BF)
    last = (GROUP - 1) * MESSAGE + EDGE
    out_ref[last - 2 * C : last, :] = jnp.zeros((2 * C, LANES), BF)
    for peer in range(GROUP):
        out_ref[(peer + 1) * MESSAGE - C : (peer + 1) * MESSAGE, :] = params_ref[...]

    def load(pair):
        rows = slice(pair * 16, pair * 16 + 16)
        both = six_planes(odd, *[ref[rows, :].astype(F32) for ref in (paired_ref, latent_ref, crossed_ref)])
        for k in range(2):
            taps[1 + pair * 2 + k] = taps_of(both[k * C : k * C + C], keeps, chosen)

    def widen(row):
        hidden[1 + row] = hidden_of(taps[row : row + 3].reshape(3 * TAPS, 4 * W), kernel_in, inside)

    def narrow(pair):
        preds = [
            predicted_of(hidden[row : row + 3].reshape(3 * HID, 4 * W), kernel_out, keeps)
            for row in (2 * pair, 2 * pair + 1)
        ]
        rows = slice(pair * 16, pair * 16 + 16)
        inc = base_ref[rows, :] + eps * jnp.concatenate(preds, axis=0)
        known = (inc - fresh_ref[rows, :]).astype(BF)
        for peer in range(GROUP):
            at = 2 * pair - (OWN * peer - 2)
            if 0 <= at < EXT:
                base = peer * MESSAGE + at * C
                out_ref[base : base + 16, :] = known if 2 <= at < 2 + OWN else inc.astype(BF)
        peer = 2 * pair // OWN
        base = peer * MESSAGE + EDGE + (2 * pair - OWN * peer) * C
        out_ref[base : base + 16, :] = (inc - known.astype(F32)).astype(BF)

    for beat in range(H // 2 + 4):
        if beat < H // 2:
            load(beat)
        if 0 <= beat - 2 < H // 2:
            widen(2 * (beat - 2))
            widen(2 * (beat - 2) + 1)
        if 0 <= beat - 4:
            narrow(beat - 4)


def scan_kernel(x_ref, before_ref, total_ref):
    for block in range(EXT // 2):
        at = block * 16
        low = at - 2 * C
        total = jnp.zeros((16, LANES), F32)
        for k in range(GROUP):
            rows = slice(k * EDGE + at, k * EDGE + at + 16)
            before_ref[rows, :] = total
            base = k * MESSAGE
            total = total + x_ref[base + at : base + at + 16, :].astype(F32)
            if 0 <= low < KEEP:
                total = total + x_ref[base + EDGE + low : base + EDGE + low + 16, :].astype(F32)
        high = total.astype(BF)
        total_ref[at : at + 16, :] = high
        if 0 <= low < KEEP:
            total_ref[EDGE + low : EDGE + low + 16, :] = (total - high.astype(F32)).astype(BF)


def state_kernel(start_ref, one_ref, two_ref, three_ref, before_ref, state_ref, latent_ref):
    for block in range(EXT // 2):
        rows = slice(block * 16, block * 16 + 16)
        low = rows.start - 2 * C
        offset = start_ref[rows, :]
        for ref in (one_ref, two_ref, three_ref):
            offset = offset + ref[rows, :].astype(F32)
            if 0 <= low < KEEP:
                offset = offset + ref[EDGE + low : EDGE + low + 16, :].astype(F32)
        for k in range(GROUP):
            at = slice(k * EDGE + rows.start, k * EDGE + rows.stop)
            state = offset + before_ref[at, :]
            latent_ref[at, :] = state.astype(BF)
            if 0 <= low < KEEP:
                state_ref[k * KEEP + low : k * KEEP + low + 16, :] = state


def tune_kernel(x_ref, spread_ref, kernel_in_ref, coefs_ref):
    params = [x_ref[(k + 1) * MESSAGE - C : (k + 1) * MESSAGE, :].astype(F32) for k in range(GROUP)]
    index = lax.broadcasted_iota(jnp.int32, (GROUP, LANES), 0)

    def gathered(row):
        out = jnp.zeros((GROUP, LANES), F32)
        for k in range(GROUP):
            out = jnp.where(index == k, params[k][row : row + 1], out)
        return out

    pieces = [
        [spread_ref[kh * TAPS + k * C : kh * TAPS + k * C + C, :] for k in range(9)] for kh in range(3)
    ]
    kernel_in_ref[...] = turned(stacked_kernel(pieces, [gathered(kh)[:, :W] for kh in range(3)]))
    coefs = gathered(3) + gathered(4) + gathered(5)
    coefs_ref[:GROUP, :] = jnp.concatenate([coefs[:, :W]] * 2, axis=1)
    coefs_ref[GROUP:, :] = jnp.concatenate([coefs[:, W:]] * 2, axis=1)


def second_step_kernel(
    slabs, paired_ref, latent_ref, crossed_ref, kernel_in_ref, kernel_out_ref, x_ref, coefs_ref, state_ref,
    sum_ref, total_ref, taps, hidden,
):
    keeps = edge_masks()
    odd, inside = slab_facts(slabs)
    part = lax.axis_index("level") % GROUP
    exists = {0: one_if(part > 0), EXT - 3: one_if(part < GROUP - 1)}
    kernel_in, kernel_out = kernel_in_ref[...], kernel_out_ref[...]
    chosen = [selector(k) for k in range(GROUP)]
    running = [jnp.zeros((16, LANES), F32) for _ in range(OWN // 2)]

    def load(level, pair):
        at = level * EDGE + pair * 16
        refs = (paired_ref, latent_ref, crossed_ref)
        both = six_planes(odd, *[ref[at : at + 16, :].astype(F32) for ref in refs])
        for k in range(2):
            taps[level * EXT + pair * 2 + k] = taps_of(both[k * C : k * C + C], keeps, chosen[level])

    def widen(level, row):
        at = level * EXT + row
        hidden[level * (EXT - 2) + row] = hidden_of(
            taps[at : at + 3].reshape(3 * TAPS, 4 * W), kernel_in, inside, exists.get(row)
        )

    def narrow(level, pair):
        at = level * (EXT - 2) + 2 * pair
        preds = [
            predicted_of(hidden[row : row + 3].reshape(3 * HID, 4 * W), kernel_out, keeps) for row in (at, at + 1)
        ]
        base = level * KEEP + pair * 16
        fresh = level * MESSAGE + EDGE + pair * 16
        inc = coefs_ref[level : level + 1, :] * state_ref[base : base + 16, :]
        inc = inc + x_ref[fresh : fresh + 16, :].astype(F32)
        inc = inc + coefs_ref[GROUP + level : GROUP + level + 1, :] * jnp.concatenate(preds, axis=0)
        running[pair] = running[pair] + inc
        sum_ref[level * KEEP + pair * 16 : level * KEEP + pair * 16 + 16, :] = running[pair]
        if level == GROUP - 1:
            total_ref[pair * 16 : pair * 16 + 16, :] = running[pair]

    for beat in range(GROUP + 2):
        loads = [(load, beat, k) for k in range(EXT // 2)] if beat < GROUP else []
        widens = [(widen, beat - 1, k) for k in range(EXT - 2)] if 0 <= beat - 1 < GROUP else []
        narrows = [(narrow, beat - 2, k) for k in range(OWN // 2)] if 0 <= beat - 2 else []
        jobs = [((k + 0.5) / len(each), job) for each in (loads, widens, narrows) for k, job in enumerate(each)]
        for _, (work, *where) in sorted(jobs, key=lambda job: job[0]):
            work(*where)


def add_kernel(start_ref, one_ref, two_ref, three_ref, sum_ref, out_ref):
    offset = start_ref[2 * C : 2 * C + KEEP, :] + (one_ref[...] + two_ref[...] + three_ref[...])
    for k in range(GROUP):
        rows = slice(k * KEEP, k * KEEP + KEEP)
        out_ref[rows, :] = offset + sum_ref[rows, :]


def final_kernel(state_ref, out_ref):
    for plane, block, rows, lanes in tiles():
        out_ref[:, plane, block * 8 : block * 8 + 8, :] = jnp.swapaxes(state_ref[rows, lanes].reshape(8, C, W), 0, 1)


VMEM = pl.BlockSpec(memory_space=pltpu.VMEM)
SMEM = pl.BlockSpec(memory_space=pltpu.SMEM)


def near(*arrays):
    return [pltpu.with_memory_space_constraint(array, pltpu.VMEM) for array in arrays]


def call(kernel, arrays, outs, scratch=(), name=None, scalars=0):
    return pl.pallas_call(
        kernel,
        out_shape=outs if len(outs) > 1 else outs[0],
        in_specs=[SMEM] * scalars + [VMEM] * (len(arrays) - scalars),
        out_specs=[VMEM] * len(outs) if len(outs) > 1 else VMEM,
        scratch_shapes=scratch,
        name=name,
    )(*arrays)


def on_device(trajectory, first_latent, noise_draw, w_in, bias_in, level_bias, w_out, bias_out, drift, eps, scale):
    slabs = lax.axis_size("slab")
    levels = lax.axis_size("level")
    pairs = [(i, i ^ 1) for i in range(slabs)]
    crossings = [(i, j) for k in range(1, slabs - 1, 2) for i, j in ((k, k + 1), (k + 1, k))]
    groups = [list(range(k, k + GROUP)) for k in range(0, levels, GROUP)]

    def neighbours(latent):
        crossed = lax.ppermute(latent, "slab", crossings)
        return lax.ppermute(latent, "slab", pairs), latent, crossed

    def exchange(array):
        parts = array.reshape(GROUP, -1, LANES)
        return lax.all_to_all(parts, "level", 0, 0, axis_index_groups=groups).reshape(array.shape)

    def earlier_groups(total):
        return [
            lax.ppermute(total, "level", [(i, i + k) for i in range(levels - k)]) for k in range(GROUP, levels, GROUP)
        ]

    latent, first_state, noise, start, kernel_in, spread, kernel_out, biases, column = call(
        opening_kernel,
        (
            trajectory[0], noise_draw[0], first_latent,
            jnp.transpose(w_in, (2, 3, 4, 1, 0)).reshape(27, C, HID), bias_in[None], level_bias,
            jnp.transpose(w_out, (2, 3, 4, 0, 1)).reshape(27, C, HID), bias_out[None],
        ),
        [
            pltpu.VMEM((H * C, LANES), BF), pltpu.VMEM((H * C, LANES), F32), pltpu.VMEM((H * C, LANES), F32),
            pltpu.VMEM((EDGE, LANES), F32), pltpu.VMEM((HID, 3 * TAPS), BF), pltpu.VMEM((3 * TAPS, W), F32),
            pltpu.VMEM((9 * C, 3 * HID), BF), pltpu.VMEM((C, W), F32), pltpu.VMEM((C, W), F32),
        ],
        [pltpu.VMEM(((H + 4) * C, LANES), F32)],
        name="opening",
    )
    base, fresh, params = call(
        prepare_kernel,
        (drift, eps, scale, *near(first_state, noise, biases, column)),
        [pltpu.VMEM((H * C, LANES), F32), pltpu.VMEM((H * C, LANES), F32), pltpu.VMEM((C, LANES), BF)],
        name="prepare",
        scalars=3,
    )
    sent = call(
        lambda *refs: first_step_kernel(slabs, *refs),
        near(*neighbours(latent), kernel_in, kernel_out, base, fresh, params),
        [pltpu.VMEM((GROUP * MESSAGE, LANES), BF)],
        [pltpu.VMEM((H + 2, TAPS, 4 * W), BF), pltpu.VMEM((H + 2, HID, 4 * W), BF)],
        name="first",
    )
    got = exchange(sent)
    before, total = call(
        scan_kernel, near(got),
        [pltpu.VMEM((GROUP * EDGE, LANES), F32), pltpu.VMEM((EDGE + KEEP, LANES), BF)], name="scan",
    )
    kernel_in, coefs = call(
        tune_kernel, near(got, spread),
        [pltpu.VMEM((HID, 3 * TAPS), BF), pltpu.VMEM((2 * GROUP, LANES), F32)], name="tune",
    )
    state, latent = call(
        state_kernel, near(start, *earlier_groups(total), before),
        [pltpu.VMEM((GROUP * KEEP, LANES), F32), pltpu.VMEM((GROUP * EDGE, LANES), BF)], name="state",
    )
    sums, total = call(
        lambda *refs: second_step_kernel(slabs, *refs),
        near(*neighbours(latent), kernel_in, kernel_out, got, coefs, state),
        [pltpu.VMEM((GROUP * KEEP, LANES), F32), pltpu.VMEM((KEEP, LANES), F32)],
        [
            pltpu.VMEM((GROUP * EXT, TAPS, 4 * W), BF),
            pltpu.VMEM((GROUP * (EXT - 2), HID, 4 * W), BF),
        ],
        name="second",
    )
    state = call(
        add_kernel, near(start, *earlier_groups(total), sums), [pltpu.VMEM((GROUP * KEEP, LANES), F32)], name="add"
    )
    return call(
        final_kernel, near(exchange(state)), [jax.ShapeDtypeStruct((C, 2, H, W), F32)], name="final"
    )[None]


def solution(mesh):
    placed = (
        P("level", None, "slab", None, None),
        P(None, "slab", None, None),
        P("level", None, "slab", None, None),
        P(),
        P(),
        P("level", None),
        P(),
        P(),
        P("level"),
        P("level"),
        P("level"),
    )
    return jax.shard_map(
        on_device,
        mesh=mesh,
        in_specs=placed,
        out_specs=P("level", None, "slab", None, None),
        check_vma=False,
    )
```

```python
import jax
import jax.numpy as jnp
from jax import lax
from jax.experimental import pallas as pl
from jax.experimental.pallas import tpu as pltpu
from jax.sharding import PartitionSpec as P

C, HID, H, W = 8, 64, 32, 128
BF, F32 = jnp.bfloat16, jnp.float32
GROUP = 8
OWN = H // GROUP
EXT = OWN + 4
LANES = 2 * W
KEEP, EDGE = OWN * C, EXT * C
MESSAGE = EDGE + KEEP + C
TAPS = 9 * C + C


def swapped(ref, plane, block):
    tile = ref[:, plane, block * 8 : block * 8 + 8, :]
    return jnp.swapaxes(tile, 0, 1).reshape(64, W)


def tiles():
    for plane in range(2):
        for block in range(4):
            yield plane, block, slice(block * 64, block * 64 + 64), slice(plane * W, plane * W + W)


def split(value, parts):
    pieces = []
    for _ in range(parts):
        pieces.append(value.astype(BF).astype(F32))
        value = value - pieces[-1]
    return pieces


def stacked_kernel(pieces, pads):
    rows = []
    for kh in range(3):
        rows += pieces[kh] + [pads[kh]]
    return jnp.concatenate(rows, axis=0)


def turned(stacked):
    spare = jnp.zeros((256 - 3 * TAPS, W), F32)
    return jnp.concatenate([stacked, spare], axis=0).T[:HID, : 3 * TAPS].astype(BF)


def opening_kernel(
    x_ref, noise_ref, first_ref, w_in_ref, bias_in_ref, level_bias_ref, w_out_ref, bias_out_ref,
    latent_ref, state_ref, noise_out_ref, start_ref, kernel_in_ref, spread_ref, kernel_out_ref, biases_ref, column_ref,
    first,
):
    edge = jnp.zeros((2 * C, LANES), F32)
    first[: 2 * C, :] = edge
    first[2 * C + H * C :, :] = edge
    for plane, block, rows, lanes in tiles():
        state = swapped(x_ref, plane, block)
        state_ref[rows, lanes] = state
        latent_ref[rows, lanes] = state.astype(BF)
        noise_out_ref[rows, lanes] = swapped(noise_ref, plane, block)
        first[rows.start + 2 * C : rows.stop + 2 * C, lanes] = swapped(first_ref, plane, block)
    own = pl.multiple_of(lax.axis_index("level") % GROUP * KEEP, KEEP)
    start_ref[...] = first[pl.ds(own, EDGE), :]

    same = lax.broadcasted_iota(jnp.int32, (C, C), 0) == lax.broadcasted_iota(jnp.int32, (C, C), 1)
    column = jnp.sum(jnp.where(same, jnp.broadcast_to(bias_out_ref[...], (C, C)), 0.0), axis=1, keepdims=True)
    column_ref[...] = jnp.broadcast_to(column, (C, W))
    bias = 0.5 * (bias_in_ref[...] + level_bias_ref[...])
    biases = split(jnp.concatenate([bias, jnp.zeros((1, W - HID), F32)], axis=1), 3)
    index = lax.broadcasted_iota(jnp.int32, (C, W), 0)
    nothing = jnp.zeros((C, W), F32)
    table = nothing
    for k, row in enumerate(biases):
        table = jnp.where(index == k, row, table)
    biases_ref[...] = table

    wide = jnp.zeros((C, W - HID), F32)
    pieces = [
        [
            jnp.concatenate([0.5 * w_in_ref[kd * 9 + kh * 3 + kw].astype(F32), wide], axis=1)
            for kd in range(3)
            for kw in range(3)
        ]
        for kh in range(3)
    ]
    spread_ref[...] = stacked_kernel(pieces, [nothing] * 3)
    kernel_in_ref[...] = turned(stacked_kernel(pieces, [jnp.where(index == 0, row, 0.0) for row in biases]))
    rows_of = [
        jnp.concatenate([w_out_ref[kd * 9 + kh * 3 + kw].astype(F32) for kd in range(3) for kw in range(3)], axis=0)
        for kh in range(3)
    ]
    kernel_out_ref[...] = jnp.concatenate(rows_of, axis=1).astype(BF)


def prepare_kernel(
    drift_ref, eps_ref, scale_ref, state_ref, noise_ref, biases_ref, column_ref, base_ref, fresh_ref, params_ref
):
    drift, eps, scale = (jnp.full((1, W), ref[0], F32) for ref in (drift_ref, eps_ref, scale_ref))
    column = eps * column_ref[...]
    shift = jnp.concatenate([column, column], axis=1)
    for row in range(H):
        rows = slice(row * C, row * C + C)
        fresh = scale_ref[0] * noise_ref[rows, :] + shift
        fresh_ref[rows, :] = fresh
        base_ref[rows, :] = drift_ref[0] * state_ref[rows, :] + fresh
    index = lax.broadcasted_iota(jnp.int32, (C, W), 0)
    left, right = biases_ref[...], jnp.zeros((C, W), F32)
    for k, row in enumerate(split(drift, 3)):
        left = jnp.where(index == 3 + k, row, left)
    for k, row in enumerate(split(eps, 3)):
        right = jnp.where(index == 3 + k, row, right)
    params_ref[...] = jnp.concatenate([left, right], axis=1).astype(BF)


def edge_masks():
    lane = lax.broadcasted_iota(jnp.int32, (C, W), 1)
    return lane > 0, lane < W - 1


def from_left(tile, keep):
    return jnp.where(keep, pltpu.roll(tile, 1, 1), 0.0)


def from_right(tile, keep):
    return jnp.where(keep, pltpu.roll(tile, W - 1, 1), 0.0)


def selector(slot):
    return jnp.where(lax.broadcasted_iota(jnp.int32, (C, 4 * W), 0) == slot, 1.0, 0.0).astype(F32)


def taps_of(row, keeps, chosen):
    blocks = [row[:, p * W : p * W + W] for p in range(6)]
    shifted = (
        [from_left(b, keeps[0]) for b in blocks],
        blocks,
        [from_right(b, keeps[1]) for b in blocks],
    )
    pieces = [jnp.concatenate(shifted[kw][kd : kd + 4], axis=1) for kd in range(3) for kw in range(3)]
    return jnp.concatenate(pieces + [chosen], axis=0).astype(BF)


def hidden_of(taps, kernel_in, inside, exists=None):
    u = jnp.dot(kernel_in, taps, preferred_element_type=F32)
    out = (u + u * jnp.tanh(u)).astype(BF)
    if exists is not None:
        out = out * jnp.concatenate([exists] * 4, axis=1)
    return jnp.concatenate([out[:, :W] * inside[0], out[:, W : 3 * W], out[:, 3 * W :] * inside[1]], axis=1)


def predicted_of(hidden, kernel_out, keeps):
    y = jnp.dot(kernel_out, hidden, preferred_element_type=F32)
    planes = []
    for plane in range(2):
        sums = []
        for kw in range(3):
            parts = [
                y[(kd * 3 + kw) * C : (kd * 3 + kw) * C + C, (plane + kd) * W : (plane + kd) * W + W]
                for kd in range(3)
            ]
            sums.append(parts[0] + parts[1] + parts[2])
        planes.append(sums[1] + from_left(sums[0], keeps[0]) + from_right(sums[2], keeps[1]))
    return jnp.concatenate(planes, axis=1)


def one_if(condition):
    return jnp.broadcast_to(jnp.where(condition, 1.0, 0.0).astype(F32), (1, W)).astype(BF)


def slab_facts(slabs):
    slab = lax.axis_index("slab")
    return slab % 2 == 1, (one_if(slab > 0), one_if(slab < slabs - 1))


def six_planes(odd, paired, own, crossed):
    below, above = jnp.where(odd, paired, crossed), jnp.where(odd, crossed, paired)
    return jnp.concatenate([below, own, above], axis=1)


def first_step_kernel(
    slabs, paired_ref, latent_ref, crossed_ref, kernel_in_ref, kernel_out_ref, base_ref, fresh_ref, params_ref,
    out_ref, taps, hidden,
):
    keeps = edge_masks()
    odd, inside = slab_facts(slabs)
    kernel_in, kernel_out = kernel_in_ref[...], kernel_out_ref[...]
    eps = sum(params_ref[...].astype(F32)[row : row + 1, W:] for row in (3, 4, 5))
    eps = jnp.concatenate([eps, eps], axis=1)
    chosen = selector(0)
    empty = jnp.concatenate([jnp.zeros((9 * C, 4 * W), F32), chosen], axis=0).astype(BF)
    for edge in (0, H + 1):
        taps[edge] = empty
        hidden[edge] = jnp.zeros((HID, 4 * W), BF)
    out_ref[: 2 * C, :] = jnp.zeros((2 * C, LANES), BF)
    last = (GROUP - 1) * MESSAGE + EDGE
    out_ref[last - 2 * C : last, :] = jnp.zeros((2 * C, LANES), BF)
    for peer in range(GROUP):
        out_ref[(peer + 1) * MESSAGE - C : (peer + 1) * MESSAGE, :] = params_ref[...]

    def load(pair):
        rows = slice(pair * 16, pair * 16 + 16)
        both = six_planes(odd, *[ref[rows, :].astype(F32) for ref in (paired_ref, latent_ref, crossed_ref)])
        for k in range(2):
            taps[1 + pair * 2 + k] = taps_of(both[k * C : k * C + C], keeps, chosen)

    def widen(row):
        hidden[1 + row] = hidden_of(taps[row : row + 3].reshape(3 * TAPS, 4 * W), kernel_in, inside)

    def narrow(pair):
        preds = [
            predicted_of(hidden[row : row + 3].reshape(3 * HID, 4 * W), kernel_out, keeps)
            for row in (2 * pair, 2 * pair + 1)
        ]
        rows = slice(pair * 16, pair * 16 + 16)
        inc = base_ref[rows, :] + eps * jnp.concatenate(preds, axis=0)
        known = (inc - fresh_ref[rows, :]).astype(BF)
        for peer in range(GROUP):
            at = 2 * pair - (OWN * peer - 2)
            if 0 <= at < EXT:
                base = peer * MESSAGE + at * C
                out_ref[base : base + 16, :] = known if 2 <= at < 2 + OWN else inc.astype(BF)
        peer = 2 * pair // OWN
        base = peer * MESSAGE + EDGE + (2 * pair - OWN * peer) * C
        out_ref[base : base + 16, :] = (inc - known.astype(F32)).astype(BF)

    for beat in range(H // 2 + 4):
        if beat < H // 2:
            load(beat)
        if 0 <= beat - 2 < H // 2:
            widen(2 * (beat - 2))
            widen(2 * (beat - 2) + 1)
        if 0 <= beat - 4:
            narrow(beat - 4)


def scan_kernel(x_ref, before_ref, total_ref):
    for block in range(EXT // 2):
        at = block * 16
        low = at - 2 * C
        total = jnp.zeros((16, LANES), F32)
        for k in range(GROUP):
            rows = slice(k * EDGE + at, k * EDGE + at + 16)
            before_ref[rows, :] = total
            base = k * MESSAGE
            total = total + x_ref[base + at : base + at + 16, :].astype(F32)
            if 0 <= low < KEEP:
                total = total + x_ref[base + EDGE + low : base + EDGE + low + 16, :].astype(F32)
        high = total.astype(BF)
        total_ref[at : at + 16, :] = high
        if 0 <= low < KEEP:
            total_ref[EDGE + low : EDGE + low + 16, :] = (total - high.astype(F32)).astype(BF)


def state_kernel(start_ref, one_ref, two_ref, three_ref, before_ref, state_ref, latent_ref):
    group = lax.axis_index("level") // GROUP
    for block in range(EXT // 2):
        rows = slice(block * 16, block * 16 + 16)
        low = rows.start - 2 * C
        offset = start_ref[rows, :]
        for k, ref in enumerate((one_ref, two_ref, three_ref)):
            total = ref[rows, :].astype(F32)
            if 0 <= low < KEEP:
                total = total + ref[EDGE + low : EDGE + low + 16, :].astype(F32)
            offset = offset + jnp.where(group > k, total, 0.0)
        for k in range(GROUP):
            at = slice(k * EDGE + rows.start, k * EDGE + rows.stop)
            state = offset + before_ref[at, :]
            latent_ref[at, :] = state.astype(BF)
            if 0 <= low < KEEP:
                state_ref[k * KEEP + low : k * KEEP + low + 16, :] = state


def tune_kernel(x_ref, spread_ref, kernel_in_ref, coefs_ref):
    params = [x_ref[(k + 1) * MESSAGE - C : (k + 1) * MESSAGE, :].astype(F32) for k in range(GROUP)]
    index = lax.broadcasted_iota(jnp.int32, (GROUP, LANES), 0)

    def gathered(row):
        out = jnp.zeros((GROUP, LANES), F32)
        for k in range(GROUP):
            out = jnp.where(index == k, params[k][row : row + 1], out)
        return out

    pieces = [
        [spread_ref[kh * TAPS + k * C : kh * TAPS + k * C + C, :] for k in range(9)] for kh in range(3)
    ]
    kernel_in_ref[...] = turned(stacked_kernel(pieces, [gathered(kh)[:, :W] for kh in range(3)]))
    coefs = gathered(3) + gathered(4) + gathered(5)
    coefs_ref[:GROUP, :] = jnp.concatenate([coefs[:, :W]] * 2, axis=1)
    coefs_ref[GROUP:, :] = jnp.concatenate([coefs[:, W:]] * 2, axis=1)


def second_step_kernel(
    slabs, paired_ref, latent_ref, crossed_ref, kernel_in_ref, kernel_out_ref, x_ref, coefs_ref, state_ref,
    sum_ref, total_ref, taps, hidden,
):
    keeps = edge_masks()
    odd, inside = slab_facts(slabs)
    part = lax.axis_index("level") % GROUP
    exists = {0: one_if(part > 0), EXT - 3: one_if(part < GROUP - 1)}
    kernel_in, kernel_out = kernel_in_ref[...], kernel_out_ref[...]
    chosen = [selector(k) for k in range(GROUP)]
    running = [jnp.zeros((16, LANES), F32) for _ in range(OWN // 2)]

    def load(level, pair):
        at = level * EDGE + pair * 16
        refs = (paired_ref, latent_ref, crossed_ref)
        both = six_planes(odd, *[ref[at : at + 16, :].astype(F32) for ref in refs])
        for k in range(2):
            taps[level * EXT + pair * 2 + k] = taps_of(both[k * C : k * C + C], keeps, chosen[level])

    def widen(level, row):
        at = level * EXT + row
        hidden[level * (EXT - 2) + row] = hidden_of(
            taps[at : at + 3].reshape(3 * TAPS, 4 * W), kernel_in, inside, exists.get(row)
        )

    def narrow(level, pair):
        at = level * (EXT - 2) + 2 * pair
        preds = [
            predicted_of(hidden[row : row + 3].reshape(3 * HID, 4 * W), kernel_out, keeps) for row in (at, at + 1)
        ]
        base = level * KEEP + pair * 16
        fresh = level * MESSAGE + EDGE + pair * 16
        inc = coefs_ref[level : level + 1, :] * state_ref[base : base + 16, :]
        inc = inc + x_ref[fresh : fresh + 16, :].astype(F32)
        inc = inc + coefs_ref[GROUP + level : GROUP + level + 1, :] * jnp.concatenate(preds, axis=0)
        running[pair] = running[pair] + inc
        sum_ref[level * KEEP + pair * 16 : level * KEEP + pair * 16 + 16, :] = running[pair]
        if level == GROUP - 1:
            total_ref[pair * 16 : pair * 16 + 16, :] = running[pair]

    for beat in range(GROUP + 2):
        loads = [(load, beat, k) for k in range(EXT // 2)] if beat < GROUP else []
        widens = [(widen, beat - 1, k) for k in range(EXT - 2)] if 0 <= beat - 1 < GROUP else []
        narrows = [(narrow, beat - 2, k) for k in range(OWN // 2)] if 0 <= beat - 2 else []
        jobs = [((k + 0.5) / len(each), job) for each in (loads, widens, narrows) for k, job in enumerate(each)]
        for _, (work, *where) in sorted(jobs, key=lambda job: job[0]):
            work(*where)


def add_kernel(start_ref, one_ref, two_ref, three_ref, sum_ref, out_ref):
    group = lax.axis_index("level") // GROUP
    refs = (one_ref, two_ref, three_ref)
    offset = start_ref[2 * C : 2 * C + KEEP, :] + sum(jnp.where(group > k, ref[...], 0.0) for k, ref in enumerate(refs))
    for k in range(GROUP):
        rows = slice(k * KEEP, k * KEEP + KEEP)
        out_ref[rows, :] = offset + sum_ref[rows, :]


def final_kernel(state_ref, out_ref):
    for plane, block, rows, lanes in tiles():
        out_ref[:, plane, block * 8 : block * 8 + 8, :] = jnp.swapaxes(state_ref[rows, lanes].reshape(8, C, W), 0, 1)


VMEM = pl.BlockSpec(memory_space=pltpu.VMEM)
SMEM = pl.BlockSpec(memory_space=pltpu.SMEM)


def near(*arrays):
    return [pltpu.with_memory_space_constraint(array, pltpu.VMEM) for array in arrays]


def call(kernel, arrays, outs, scratch=(), name=None, scalars=0):
    return pl.pallas_call(
        kernel,
        out_shape=outs if len(outs) > 1 else outs[0],
        in_specs=[SMEM] * scalars + [VMEM] * (len(arrays) - scalars),
        out_specs=[VMEM] * len(outs) if len(outs) > 1 else VMEM,
        scratch_shapes=scratch,
        name=name,
    )(*arrays)


def on_device(trajectory, first_latent, noise_draw, w_in, bias_in, level_bias, w_out, bias_out, drift, eps, scale):
    slabs = lax.axis_size("slab")
    levels = lax.axis_size("level")
    pairs = [(i, i ^ 1) for i in range(slabs)]
    crossings = [(i, j) for k in range(1, slabs - 1, 2) for i, j in ((k, k + 1), (k + 1, k))]
    groups = [list(range(k, k + GROUP)) for k in range(0, levels, GROUP)]

    def neighbours(latent):
        crossed = lax.ppermute(latent, "slab", crossings)
        return lax.ppermute(latent, "slab", pairs), latent, crossed

    def exchange(array):
        parts = array.reshape(GROUP, -1, LANES)
        return lax.all_to_all(parts, "level", 0, 0, axis_index_groups=groups).reshape(array.shape)

    def earlier_groups(total):
        return [
            lax.ppermute(total, "level", [(i, (i + k) % levels) for i in range(levels)])
            for k in range(GROUP, levels, GROUP)
        ]

    latent, first_state, noise, start, kernel_in, spread, kernel_out, biases, column = call(
        opening_kernel,
        (
            trajectory[0], noise_draw[0], first_latent,
            jnp.transpose(w_in, (2, 3, 4, 1, 0)).reshape(27, C, HID), bias_in[None], level_bias,
            jnp.transpose(w_out, (2, 3, 4, 0, 1)).reshape(27, C, HID), bias_out[None],
        ),
        [
            pltpu.VMEM((H * C, LANES), BF), pltpu.VMEM((H * C, LANES), F32), pltpu.VMEM((H * C, LANES), F32),
            pltpu.VMEM((EDGE, LANES), F32), pltpu.VMEM((HID, 3 * TAPS), BF), pltpu.VMEM((3 * TAPS, W), F32),
            pltpu.VMEM((9 * C, 3 * HID), BF), pltpu.VMEM((C, W), F32), pltpu.VMEM((C, W), F32),
        ],
        [pltpu.VMEM(((H + 4) * C, LANES), F32)],
        name="opening",
    )
    base, fresh, params = call(
        prepare_kernel,
        (drift, eps, scale, *near(first_state, noise, biases, column)),
        [pltpu.VMEM((H * C, LANES), F32), pltpu.VMEM((H * C, LANES), F32), pltpu.VMEM((C, LANES), BF)],
        name="prepare",
        scalars=3,
    )
    sent = call(
        lambda *refs: first_step_kernel(slabs, *refs),
        near(*neighbours(latent), kernel_in, kernel_out, base, fresh, params),
        [pltpu.VMEM((GROUP * MESSAGE, LANES), BF)],
        [pltpu.VMEM((H + 2, TAPS, 4 * W), BF), pltpu.VMEM((H + 2, HID, 4 * W), BF)],
        name="first",
    )
    got = exchange(sent)
    before, total = call(
        scan_kernel, near(got),
        [pltpu.VMEM((GROUP * EDGE, LANES), F32), pltpu.VMEM((EDGE + KEEP, LANES), BF)], name="scan",
    )
    kernel_in, coefs = call(
        tune_kernel, near(got, spread),
        [pltpu.VMEM((HID, 3 * TAPS), BF), pltpu.VMEM((2 * GROUP, LANES), F32)], name="tune",
    )
    state, latent = call(
        state_kernel, near(start, *earlier_groups(total), before),
        [pltpu.VMEM((GROUP * KEEP, LANES), F32), pltpu.VMEM((GROUP * EDGE, LANES), BF)], name="state",
    )
    sums, total = call(
        lambda *refs: second_step_kernel(slabs, *refs),
        near(*neighbours(latent), kernel_in, kernel_out, got, coefs, state),
        [pltpu.VMEM((GROUP * KEEP, LANES), F32), pltpu.VMEM((KEEP, LANES), F32)],
        [
            pltpu.VMEM((GROUP * EXT, TAPS, 4 * W), BF),
            pltpu.VMEM((GROUP * (EXT - 2), HID, 4 * W), BF),
        ],
        name="second",
    )
    state = call(
        add_kernel, near(start, *earlier_groups(total), sums), [pltpu.VMEM((GROUP * KEEP, LANES), F32)], name="add"
    )
    return call(
        final_kernel, near(exchange(state)), [jax.ShapeDtypeStruct((C, 2, H, W), F32)], name="final"
    )[None]


def solution(mesh):
    placed = (
        P("level", None, "slab", None, None),
        P(None, "slab", None, None),
        P("level", None, "slab", None, None),
        P(),
        P(),
        P("level", None),
        P(),
        P(),
        P("level"),
        P("level"),
        P("level"),
    )
    return jax.shard_map(
        on_device,
        mesh=mesh,
        in_specs=placed,
        out_specs=P("level", None, "slab", None, None),
        check_vma=False,
    )
```

```python
import jax
import jax.numpy as jnp
from jax import lax
from jax.experimental import pallas as pl
from jax.experimental.pallas import tpu as pltpu
from jax.sharding import PartitionSpec as P

C, HID, H, W = 8, 64, 32, 128
BF, F32 = jnp.bfloat16, jnp.float32
GROUP = 8
OWN = H // GROUP
EXT = OWN + 4
LANES = 2 * W
KEEP, EDGE = OWN * C, EXT * C
MESSAGE = EDGE + KEEP + C
TAPS = 9 * C + C


def swapped(ref, plane, block):
    tile = ref[:, plane, block * 8 : block * 8 + 8, :]
    return jnp.swapaxes(tile, 0, 1).reshape(64, W)


def tiles():
    for plane in range(2):
        for block in range(4):
            yield plane, block, slice(block * 64, block * 64 + 64), slice(plane * W, plane * W + W)


def split(value, parts):
    pieces = []
    for _ in range(parts):
        pieces.append(value.astype(BF).astype(F32))
        value = value - pieces[-1]
    return pieces


def stacked_kernel(pieces, pads):
    rows = []
    for kh in range(3):
        rows += pieces[kh] + [pads[kh]]
    return jnp.concatenate(rows, axis=0)


def turned(stacked):
    spare = jnp.zeros((256 - 3 * TAPS, W), F32)
    return jnp.concatenate([stacked, spare], axis=0).T[:HID, : 3 * TAPS].astype(BF)


def opening_kernel(
    x_ref, noise_ref, first_ref, w_in_ref, bias_in_ref, level_bias_ref, w_out_ref, bias_out_ref,
    latent_ref, state_ref, noise_out_ref, start_ref, kernel_in_ref, spread_ref, kernel_out_ref, biases_ref, column_ref,
    first,
):
    edge = jnp.zeros((2 * C, LANES), F32)
    first[: 2 * C, :] = edge
    first[2 * C + H * C :, :] = edge
    for plane, block, rows, lanes in tiles():
        state = swapped(x_ref, plane, block)
        state_ref[rows, lanes] = state
        latent_ref[rows, lanes] = state.astype(BF)
        noise_out_ref[rows, lanes] = swapped(noise_ref, plane, block)
        first[rows.start + 2 * C : rows.stop + 2 * C, lanes] = swapped(first_ref, plane, block)
    own = pl.multiple_of(lax.axis_index("level") % GROUP * KEEP, KEEP)
    start_ref[...] = first[pl.ds(own, EDGE), :]

    same = lax.broadcasted_iota(jnp.int32, (C, C), 0) == lax.broadcasted_iota(jnp.int32, (C, C), 1)
    column = jnp.sum(jnp.where(same, jnp.broadcast_to(bias_out_ref[...], (C, C)), 0.0), axis=1, keepdims=True)
    column_ref[...] = jnp.broadcast_to(column, (C, W))
    bias = 0.5 * (bias_in_ref[...] + level_bias_ref[...])
    biases = split(jnp.concatenate([bias, jnp.zeros((1, W - HID), F32)], axis=1), 3)
    index = lax.broadcasted_iota(jnp.int32, (C, W), 0)
    nothing = jnp.zeros((C, W), F32)
    table = nothing
    for k, row in enumerate(biases):
        table = jnp.where(index == k, row, table)
    biases_ref[...] = table

    wide = jnp.zeros((C, W - HID), F32)
    pieces = [
        [
            jnp.concatenate([0.5 * w_in_ref[kd * 9 + kh * 3 + kw].astype(F32), wide], axis=1)
            for kd in range(3)
            for kw in range(3)
        ]
        for kh in range(3)
    ]
    spread_ref[...] = stacked_kernel(pieces, [nothing] * 3)
    kernel_in_ref[...] = turned(stacked_kernel(pieces, [jnp.where(index == 0, row, 0.0) for row in biases]))
    rows_of = [
        jnp.concatenate([w_out_ref[kd * 9 + kh * 3 + kw].astype(F32) for kd in range(3) for kw in range(3)], axis=0)
        for kh in range(3)
    ]
    kernel_out_ref[...] = jnp.concatenate(rows_of, axis=1).astype(BF)


def prepare_kernel(
    drift_ref, eps_ref, scale_ref, state_ref, noise_ref, biases_ref, column_ref, base_ref, fresh_ref, params_ref
):
    drift, eps, scale = (jnp.full((1, W), ref[0], F32) for ref in (drift_ref, eps_ref, scale_ref))
    column = eps * column_ref[...]
    shift = jnp.concatenate([column, column], axis=1)
    for row in range(H):
        rows = slice(row * C, row * C + C)
        fresh = scale_ref[0] * noise_ref[rows, :] + shift
        fresh_ref[rows, :] = fresh
        base_ref[rows, :] = drift_ref[0] * state_ref[rows, :] + fresh
    index = lax.broadcasted_iota(jnp.int32, (C, W), 0)
    left, right = biases_ref[...], jnp.zeros((C, W), F32)
    for k, row in enumerate(split(drift, 3)):
        left = jnp.where(index == 3 + k, row, left)
    for k, row in enumerate(split(eps, 3)):
        right = jnp.where(index == 3 + k, row, right)
    params_ref[...] = jnp.concatenate([left, right], axis=1).astype(BF)


def edge_masks():
    lane = lax.broadcasted_iota(jnp.int32, (C, W), 1)
    return lane > 0, lane < W - 1


def from_left(tile, keep):
    return jnp.where(keep, pltpu.roll(tile, 1, 1), 0.0)


def from_right(tile, keep):
    return jnp.where(keep, pltpu.roll(tile, W - 1, 1), 0.0)


def selector(slot):
    return jnp.where(lax.broadcasted_iota(jnp.int32, (C, 4 * W), 0) == slot, 1.0, 0.0).astype(F32)


def taps_of(row, keeps, chosen):
    blocks = [row[:, p * W : p * W + W] for p in range(6)]
    shifted = (
        [from_left(b, keeps[0]) for b in blocks],
        blocks,
        [from_right(b, keeps[1]) for b in blocks],
    )
    pieces = [jnp.concatenate(shifted[kw][kd : kd + 4], axis=1) for kd in range(3) for kw in range(3)]
    return jnp.concatenate(pieces + [chosen], axis=0).astype(BF)


def hidden_of(taps, kernel_in, inside, exists=None):
    u = jnp.dot(kernel_in, taps, preferred_element_type=F32)
    out = (u + u * jnp.tanh(u)).astype(BF)
    if exists is not None:
        out = out * jnp.concatenate([exists] * 4, axis=1)
    return jnp.concatenate([out[:, :W] * inside[0], out[:, W : 3 * W], out[:, 3 * W :] * inside[1]], axis=1)


def predicted_of(hidden, kernel_out, keeps):
    y = jnp.dot(kernel_out, hidden, preferred_element_type=F32)
    planes = []
    for plane in range(2):
        sums = []
        for kw in range(3):
            parts = [
                y[(kd * 3 + kw) * C : (kd * 3 + kw) * C + C, (plane + kd) * W : (plane + kd) * W + W]
                for kd in range(3)
            ]
            sums.append(parts[0] + parts[1] + parts[2])
        planes.append(sums[1] + from_left(sums[0], keeps[0]) + from_right(sums[2], keeps[1]))
    return jnp.concatenate(planes, axis=1)


def one_if(condition):
    return jnp.broadcast_to(jnp.where(condition, 1.0, 0.0).astype(F32), (1, W)).astype(BF)


def slab_facts(slabs):
    slab = lax.axis_index("slab")
    return (slab % 2 == 1, (slab > 0) & (slab < slabs - 1)), (one_if(slab > 0), one_if(slab < slabs - 1))


def six_planes(place, paired, own, crossed):
    odd, between = place
    crossed = jnp.where(between, crossed, 0.0)
    below, above = jnp.where(odd, paired, crossed), jnp.where(odd, crossed, paired)
    return jnp.concatenate([below, own, above], axis=1)


def first_step_kernel(
    slabs, paired_ref, latent_ref, crossed_ref, kernel_in_ref, kernel_out_ref, base_ref, fresh_ref, params_ref,
    out_ref, taps, hidden,
):
    keeps = edge_masks()
    place, inside = slab_facts(slabs)
    kernel_in, kernel_out = kernel_in_ref[...], kernel_out_ref[...]
    eps = sum(params_ref[...].astype(F32)[row : row + 1, W:] for row in (3, 4, 5))
    eps = jnp.concatenate([eps, eps], axis=1)
    chosen = selector(0)
    empty = jnp.concatenate([jnp.zeros((9 * C, 4 * W), F32), chosen], axis=0).astype(BF)
    for edge in (0, H + 1):
        taps[edge] = empty
        hidden[edge] = jnp.zeros((HID, 4 * W), BF)
    out_ref[: 2 * C, :] = jnp.zeros((2 * C, LANES), BF)
    last = (GROUP - 1) * MESSAGE + EDGE
    out_ref[last - 2 * C : last, :] = jnp.zeros((2 * C, LANES), BF)
    for peer in range(GROUP):
        out_ref[(peer + 1) * MESSAGE - C : (peer + 1) * MESSAGE, :] = params_ref[...]

    def load(pair):
        rows = slice(pair * 16, pair * 16 + 16)
        both = six_planes(place, *[ref[rows, :].astype(F32) for ref in (paired_ref, latent_ref, crossed_ref)])
        for k in range(2):
            taps[1 + pair * 2 + k] = taps_of(both[k * C : k * C + C], keeps, chosen)

    def widen(row):
        hidden[1 + row] = hidden_of(taps[row : row + 3].reshape(3 * TAPS, 4 * W), kernel_in, inside)

    def narrow(pair):
        preds = [
            predicted_of(hidden[row : row + 3].reshape(3 * HID, 4 * W), kernel_out, keeps)
            for row in (2 * pair, 2 * pair + 1)
        ]
        rows = slice(pair * 16, pair * 16 + 16)
        inc = base_ref[rows, :] + eps * jnp.concatenate(preds, axis=0)
        known = (inc - fresh_ref[rows, :]).astype(BF)
        for peer in range(GROUP):
            at = 2 * pair - (OWN * peer - 2)
            if 0 <= at < EXT:
                base = peer * MESSAGE + at * C
                out_ref[base : base + 16, :] = known if 2 <= at < 2 + OWN else inc.astype(BF)
        peer = 2 * pair // OWN
        base = peer * MESSAGE + EDGE + (2 * pair - OWN * peer) * C
        out_ref[base : base + 16, :] = (inc - known.astype(F32)).astype(BF)

    for beat in range(H // 2 + 4):
        if beat < H // 2:
            load(beat)
        if 0 <= beat - 2 < H // 2:
            widen(2 * (beat - 2))
            widen(2 * (beat - 2) + 1)
        if 0 <= beat - 4:
            narrow(beat - 4)


def scan_kernel(x_ref, before_ref, total_ref):
    for block in range(EXT // 2):
        at = block * 16
        low = at - 2 * C
        total = jnp.zeros((16, LANES), F32)
        for k in range(GROUP):
            rows = slice(k * EDGE + at, k * EDGE + at + 16)
            before_ref[rows, :] = total
            base = k * MESSAGE
            total = total + x_ref[base + at : base + at + 16, :].astype(F32)
            if 0 <= low < KEEP:
                total = total + x_ref[base + EDGE + low : base + EDGE + low + 16, :].astype(F32)
        high = total.astype(BF)
        total_ref[at : at + 16, :] = high
        if 0 <= low < KEEP:
            total_ref[EDGE + low : EDGE + low + 16, :] = (total - high.astype(F32)).astype(BF)


def state_kernel(start_ref, one_ref, two_ref, three_ref, before_ref, state_ref, latent_ref):
    group = lax.axis_index("level") // GROUP
    for block in range(EXT // 2):
        rows = slice(block * 16, block * 16 + 16)
        low = rows.start - 2 * C
        offset = start_ref[rows, :]
        for k, ref in enumerate((one_ref, two_ref, three_ref)):
            total = ref[rows, :].astype(F32)
            if 0 <= low < KEEP:
                total = total + ref[EDGE + low : EDGE + low + 16, :].astype(F32)
            offset = offset + jnp.where(group > k, total, 0.0)
        for k in range(GROUP):
            at = slice(k * EDGE + rows.start, k * EDGE + rows.stop)
            state = offset + before_ref[at, :]
            latent_ref[at, :] = state.astype(BF)
            if 0 <= low < KEEP:
                state_ref[k * KEEP + low : k * KEEP + low + 16, :] = state


def tune_kernel(x_ref, spread_ref, kernel_in_ref, coefs_ref):
    params = [x_ref[(k + 1) * MESSAGE - C : (k + 1) * MESSAGE, :].astype(F32) for k in range(GROUP)]
    index = lax.broadcasted_iota(jnp.int32, (GROUP, LANES), 0)

    def gathered(row):
        out = jnp.zeros((GROUP, LANES), F32)
        for k in range(GROUP):
            out = jnp.where(index == k, params[k][row : row + 1], out)
        return out

    pieces = [
        [spread_ref[kh * TAPS + k * C : kh * TAPS + k * C + C, :] for k in range(9)] for kh in range(3)
    ]
    kernel_in_ref[...] = turned(stacked_kernel(pieces, [gathered(kh)[:, :W] for kh in range(3)]))
    coefs = gathered(3) + gathered(4) + gathered(5)
    coefs_ref[:GROUP, :] = jnp.concatenate([coefs[:, :W]] * 2, axis=1)
    coefs_ref[GROUP:, :] = jnp.concatenate([coefs[:, W:]] * 2, axis=1)


def second_step_kernel(
    slabs, paired_ref, latent_ref, crossed_ref, kernel_in_ref, kernel_out_ref, x_ref, coefs_ref, state_ref,
    sum_ref, total_ref, taps, hidden,
):
    keeps = edge_masks()
    place, inside = slab_facts(slabs)
    part = lax.axis_index("level") % GROUP
    exists = {0: one_if(part > 0), EXT - 3: one_if(part < GROUP - 1)}
    kernel_in, kernel_out = kernel_in_ref[...], kernel_out_ref[...]
    chosen = [selector(k) for k in range(GROUP)]
    running = [jnp.zeros((16, LANES), F32) for _ in range(OWN // 2)]

    def load(level, pair):
        at = level * EDGE + pair * 16
        refs = (paired_ref, latent_ref, crossed_ref)
        both = six_planes(place, *[ref[at : at + 16, :].astype(F32) for ref in refs])
        for k in range(2):
            taps[level * EXT + pair * 2 + k] = taps_of(both[k * C : k * C + C], keeps, chosen[level])

    def widen(level, row):
        at = level * EXT + row
        hidden[level * (EXT - 2) + row] = hidden_of(
            taps[at : at + 3].reshape(3 * TAPS, 4 * W), kernel_in, inside, exists.get(row)
        )

    def narrow(level, pair):
        at = level * (EXT - 2) + 2 * pair
        preds = [
            predicted_of(hidden[row : row + 3].reshape(3 * HID, 4 * W), kernel_out, keeps) for row in (at, at + 1)
        ]
        base = level * KEEP + pair * 16
        fresh = level * MESSAGE + EDGE + pair * 16
        inc = coefs_ref[level : level + 1, :] * state_ref[base : base + 16, :]
        inc = inc + x_ref[fresh : fresh + 16, :].astype(F32)
        inc = inc + coefs_ref[GROUP + level : GROUP + level + 1, :] * jnp.concatenate(preds, axis=0)
        running[pair] = running[pair] + inc
        sum_ref[level * KEEP + pair * 16 : level * KEEP + pair * 16 + 16, :] = running[pair]
        if level == GROUP - 1:
            total_ref[pair * 16 : pair * 16 + 16, :] = running[pair]

    for beat in range(GROUP + 2):
        loads = [(load, beat, k) for k in range(EXT // 2)] if beat < GROUP else []
        widens = [(widen, beat - 1, k) for k in range(EXT - 2)] if 0 <= beat - 1 < GROUP else []
        narrows = [(narrow, beat - 2, k) for k in range(OWN // 2)] if 0 <= beat - 2 else []
        jobs = [((k + 0.5) / len(each), job) for each in (loads, widens, narrows) for k, job in enumerate(each)]
        for _, (work, *where) in sorted(jobs, key=lambda job: job[0]):
            work(*where)


def add_kernel(start_ref, one_ref, two_ref, three_ref, sum_ref, out_ref):
    group = lax.axis_index("level") // GROUP
    refs = (one_ref, two_ref, three_ref)
    offset = start_ref[2 * C : 2 * C + KEEP, :] + sum(jnp.where(group > k, ref[...], 0.0) for k, ref in enumerate(refs))
    for k in range(GROUP):
        rows = slice(k * KEEP, k * KEEP + KEEP)
        out_ref[rows, :] = offset + sum_ref[rows, :]


def final_kernel(state_ref, out_ref):
    for plane, block, rows, lanes in tiles():
        out_ref[:, plane, block * 8 : block * 8 + 8, :] = jnp.swapaxes(state_ref[rows, lanes].reshape(8, C, W), 0, 1)


VMEM = pl.BlockSpec(memory_space=pltpu.VMEM)
SMEM = pl.BlockSpec(memory_space=pltpu.SMEM)


def near(*arrays):
    return [pltpu.with_memory_space_constraint(array, pltpu.VMEM) for array in arrays]


def call(kernel, arrays, outs, scratch=(), name=None, scalars=0):
    return pl.pallas_call(
        kernel,
        out_shape=outs if len(outs) > 1 else outs[0],
        in_specs=[SMEM] * scalars + [VMEM] * (len(arrays) - scalars),
        out_specs=[VMEM] * len(outs) if len(outs) > 1 else VMEM,
        scratch_shapes=scratch,
        name=name,
    )(*arrays)


def on_device(trajectory, first_latent, noise_draw, w_in, bias_in, level_bias, w_out, bias_out, drift, eps, scale):
    slabs = lax.axis_size("slab")
    levels = lax.axis_size("level")
    pairs = [(i, i ^ 1) for i in range(slabs)]
    crossings = [(i, (i + (1 if i % 2 else -1)) % slabs) for i in range(slabs)]
    groups = [list(range(k, k + GROUP)) for k in range(0, levels, GROUP)]

    def neighbours(latent):
        crossed = lax.ppermute(latent, "slab", crossings)
        return lax.ppermute(latent, "slab", pairs), latent, crossed

    def exchange(array):
        parts = array.reshape(GROUP, -1, LANES)
        return lax.all_to_all(parts, "level", 0, 0, axis_index_groups=groups).reshape(array.shape)

    def earlier_groups(total):
        return [
            lax.ppermute(total, "level", [(i, (i + k) % levels) for i in range(levels)])
            for k in range(GROUP, levels, GROUP)
        ]

    latent, first_state, noise, start, kernel_in, spread, kernel_out, biases, column = call(
        opening_kernel,
        (
            trajectory[0], noise_draw[0], first_latent,
            jnp.transpose(w_in, (2, 3, 4, 1, 0)).reshape(27, C, HID), bias_in[None], level_bias,
            jnp.transpose(w_out, (2, 3, 4, 0, 1)).reshape(27, C, HID), bias_out[None],
        ),
        [
            pltpu.VMEM((H * C, LANES), BF), pltpu.VMEM((H * C, LANES), F32), pltpu.VMEM((H * C, LANES), F32),
            pltpu.VMEM((EDGE, LANES), F32), pltpu.VMEM((HID, 3 * TAPS), BF), pltpu.VMEM((3 * TAPS, W), F32),
            pltpu.VMEM((9 * C, 3 * HID), BF), pltpu.VMEM((C, W), F32), pltpu.VMEM((C, W), F32),
        ],
        [pltpu.VMEM(((H + 4) * C, LANES), F32)],
        name="opening",
    )
    base, fresh, params = call(
        prepare_kernel,
        (drift, eps, scale, *near(first_state, noise, biases, column)),
        [pltpu.VMEM((H * C, LANES), F32), pltpu.VMEM((H * C, LANES), F32), pltpu.VMEM((C, LANES), BF)],
        name="prepare",
        scalars=3,
    )
    sent = call(
        lambda *refs: first_step_kernel(slabs, *refs),
        near(*neighbours(latent), kernel_in, kernel_out, base, fresh, params),
        [pltpu.VMEM((GROUP * MESSAGE, LANES), BF)],
        [pltpu.VMEM((H + 2, TAPS, 4 * W), BF), pltpu.VMEM((H + 2, HID, 4 * W), BF)],
        name="first",
    )
    got = exchange(sent)
    before, total = call(
        scan_kernel, near(got),
        [pltpu.VMEM((GROUP * EDGE, LANES), F32), pltpu.VMEM((EDGE + KEEP, LANES), BF)], name="scan",
    )
    kernel_in, coefs = call(
        tune_kernel, near(got, spread),
        [pltpu.VMEM((HID, 3 * TAPS), BF), pltpu.VMEM((2 * GROUP, LANES), F32)], name="tune",
    )
    state, latent = call(
        state_kernel, near(start, *earlier_groups(total), before),
        [pltpu.VMEM((GROUP * KEEP, LANES), F32), pltpu.VMEM((GROUP * EDGE, LANES), BF)], name="state",
    )
    sums, total = call(
        lambda *refs: second_step_kernel(slabs, *refs),
        near(*neighbours(latent), kernel_in, kernel_out, got, coefs, state),
        [pltpu.VMEM((GROUP * KEEP, LANES), F32), pltpu.VMEM((KEEP, LANES), F32)],
        [
            pltpu.VMEM((GROUP * EXT, TAPS, 4 * W), BF),
            pltpu.VMEM((GROUP * (EXT - 2), HID, 4 * W), BF),
        ],
        name="second",
    )
    state = call(
        add_kernel, near(start, *earlier_groups(total), sums), [pltpu.VMEM((GROUP * KEEP, LANES), F32)], name="add"
    )
    return call(
        final_kernel, near(exchange(state)), [jax.ShapeDtypeStruct((C, 2, H, W), F32)], name="final"
    )[None]


def solution(mesh):
    placed = (
        P("level", None, "slab", None, None),
        P(None, "slab", None, None),
        P("level", None, "slab", None, None),
        P(),
        P(),
        P("level", None),
        P(),
        P(),
        P("level"),
        P("level"),
        P("level"),
    )
    return jax.shard_map(
        on_device,
        mesh=mesh,
        in_specs=placed,
        out_specs=P("level", None, "slab", None, None),
        check_vma=False,
    )
```
